32 devices in a mesh: groups: 2 (over y), seq: 1, mp: 8 (over z, x), section: 2 (over core).
Axes of the slice: x: 2, y: 2, z: 4, core: 2. Of those that a mesh axis runs over, the one named last changes fastest.
Arguments:
- latent: bfloat16 [1024, 3072], P(('groups', 'seq', 'section'), 'mp'), parts along dimension 0, may hold values from -6 to 6
- t_index: int32 [2], P('groups'), parts along dimension 0, may hold values from 0 to 27
- mod_table: bfloat16 [28, 3, 3072], P(None, None, 'mp'), may hold values from -1 to 4
- w_qkv: bfloat16 [3072, 6144], P('section', 'mp'), may hold values from -1 to 1
- w_out: bfloat16 [2048, 3072], P('section', 'mp'), may hold values from -0.125 to 0.125
Outputs:
- updated: bfloat16 [1024, 3072], P(('groups', 'seq', 'section'), 'mp'), parts along dimension 0
The draws below stay inside these ranges and needn't reach their ends.
There are 2 independent parts, one for each index of `groups`. The reference program is written for one: setup_inputs(seed, part) draws one part's arguments, and reference() takes and returns one part's arrays. A program takes and returns all parts, laid end to end along the dimension named above; an argument that names none is the same for every part. Nothing has to cross between parts.
Inputs may be any that keep to these rules, and one draw needn't show every extreme that they name: `t_index`: the index of the current step among 28.
All inputs are finite; a program needn't handle non-finite values.
Results may differ from the reference program's by a relative error of at most 0.0085.
The reference program's roundings to bfloat16 on the way (of `modulated`, `projected` and `attended`) count: a program that leaves them out, or rounds other values in their place, can miss the bound.
Values may be sent and summed in bfloat16 or wider, within the bound.
A program may use at most 128 MiB of HBM per device.

```python
import math
import jax
import jax.numpy as jnp
from jax import lax

D = 3072
HEADS = 16
HEAD_DIM = 128
STEPS = 28
SEQ_LEN = 512


def draw_latent(key, part):
    key_own = jax.random.fold_in(key, 11)
    own = jax.random.normal(key_own, (SEQ_LEN, D), jnp.float32)
    return jnp.clip(own, -6.0, 6.0).astype(jnp.bfloat16)


def draw_mod_table(key, part):
    key_shift, key_scale, key_gate = jax.random.split(key, 3)
    shift_rows = jax.random.uniform(key_shift, (STEPS, 1, D), jnp.float32, -1.0, 1.0)
    scale_rows = jax.random.uniform(key_scale, (STEPS, 1, D), jnp.float32, -0.5, 4.0)
    gate_rows = jax.random.uniform(key_gate, (STEPS, 1, D), jnp.float32, 0.5, 2.0)
    return jnp.concatenate([shift_rows, scale_rows, gate_rows], axis=1).astype(jnp.bfloat16)


def draw_w_qkv(key, part):
    key_values = jax.random.fold_in(jax.random.fold_in(key, 23), 0)
    raw_values = jnp.clip(jax.random.normal(key_values, (D, HEADS, 3, HEAD_DIM), jnp.float32), -6.0, 6.0)
    aligned = raw_values[:, :, 1]
    raw_values = jnp.stack([raw_values[:, :, 0], aligned, raw_values[:, :, 2]], axis=2)
    return (raw_values.reshape(D, HEADS * 3 * HEAD_DIM) / math.sqrt(D)).astype(jnp.bfloat16)


def shard_levels(rng, extent, pieces, least, largest):
    def one(position, parts):
        draws = jax.random.uniform(jax.random.fold_in(jax.random.fold_in(rng, 6), position), (parts,), jnp.float32, least / len(pieces), largest / len(pieces))
        return jnp.repeat(jnp.exp(draws), extent[position] // parts).reshape((-1,) + (1,) * (len(extent) - position - 1))

    factor_of = one(*pieces[0])
    for cut in pieces[1:]:
        factor_of = factor_of * one(*cut)
    return factor_of


def bell_draw(own_key, dims, spread, reach, cuts=(), kind=jnp.bfloat16):
    loudness = shard_levels(own_key, dims, cuts, -0.22, 0.18) if cuts else 1.0
    result = jax.random.normal(own_key, dims, jnp.float32) * spread * loudness
    return jnp.minimum(jnp.maximum(result, -reach), reach).astype(kind)


def setup_inputs(seed: int = 0, part: int = 0) -> dict:
    streams_of = jax.random.split(jax.random.key(seed), 6)
    own_keys = jax.random.split(jax.random.fold_in(streams_of[5], part), 6)
    latent = draw_latent(jax.random.fold_in(jax.random.fold_in(streams_of[5], part), 71), part)
    t_index = jax.random.randint(own_keys[1], (1,), 0, STEPS).astype(jnp.int32)
    mod_table = draw_mod_table(jax.random.fold_in(streams_of[5], 71), part)
    w_qkv = draw_w_qkv(jax.random.fold_in(streams_of[5], 71), part)
    w_out = bell_draw(streams_of[4], (HEADS * HEAD_DIM, D), (HEADS * HEAD_DIM) ** -0.5, 0.125, ((0, 2), (1, 8)))
    return {"latent": latent, "t_index": t_index, "mod_table": mod_table, "w_qkv": w_qkv, "w_out": w_out}


def layer_normed(values):
    mean_row = lax.optimization_barrier(jnp.mean(values, axis=-1, keepdims=True))
    centred = values - mean_row
    variance = lax.optimization_barrier(jnp.mean(centred * centred, axis=-1, keepdims=True))
    return centred * lax.rsqrt(variance + 1e-06)

def one_head(head_parts):
    queries = head_parts[0]
    key_rows = head_parts[1]
    value_rows = head_parts[2]
    scores = jnp.dot(queries, key_rows.T, preferred_element_type=jnp.float32) * (1.0 / math.sqrt(HEAD_DIM))
    weights = jnp.exp(scores - lax.optimization_barrier(jnp.max(scores, axis=-1, keepdims=True)))
    numerator = jnp.dot(weights.astype(jnp.bfloat16), value_rows, preferred_element_type=jnp.float32)
    return (numerator / lax.optimization_barrier(jnp.sum(weights, axis=-1, keepdims=True))).astype(jnp.bfloat16)

def reference(latent, t_index, mod_table, w_qkv, w_out):
    mod_row = lax.dynamic_index_in_dim(mod_table, t_index[0], 0, keepdims=False).astype(jnp.float32)
    base = latent.astype(jnp.float32)
    modulated = (layer_normed(base) * (1.0 + mod_row[1]) + mod_row[0]).astype(jnp.bfloat16)
    projected = jnp.dot(modulated, w_qkv, preferred_element_type=jnp.float32).astype(jnp.bfloat16)
    token_count = projected.shape[0]
    grouped = projected.reshape(token_count, HEADS, 3, HEAD_DIM).transpose(1, 2, 0, 3)
    attended = lax.map(one_head, grouped)
    flat = attended.transpose(1, 0, 2).reshape(token_count, HEADS * HEAD_DIM)
    mixed_rows = jnp.dot(flat, w_out, preferred_element_type=jnp.float32)
    return (base + mod_row[2] * mixed_rows).astype(jnp.bfloat16)
```

```python
import functools
import math

import jax
import jax.numpy as jnp
from jax import lax
from jax.experimental import pallas as pl
from jax.experimental.pallas import tpu as pltpu
from jax.sharding import PartitionSpec as P

HEAD_DIM = 128
LANES = 128
WIDE = 2
MESH = pl.DeviceIdType.MESH


def layer_normed(values):
    mean_row = jnp.mean(values, axis=-1, keepdims=True)
    centred = values - mean_row
    variance = jnp.mean(centred * centred, axis=-1, keepdims=True)
    return centred * lax.rsqrt(variance + 1e-06)


def local(latent, t_index, mod_table, w_qkv, w_out):
    mod_local = lax.dynamic_index_in_dim(mod_table, t_index[0], 0, keepdims=False)
    features, mod_whole = (
        lax.all_gather(latent, "mp", axis=1, tiled=True),
        lax.all_gather(mod_local, "mp", axis=1, tiled=True),
    )
    mod_float = mod_whole.astype(jnp.float32)
    modulated = (
        layer_normed(features.astype(jnp.float32)) * (1.0 + mod_float[1]) + mod_float[0]
    ).astype(jnp.bfloat16)
    tok_rows = latent.shape[0]
    heads_dev = w_qkv.shape[1] // (3 * HEAD_DIM)
    qkv_full, out_full = (
        lax.all_gather(w_qkv, "section", axis=0, tiled=True),
        lax.all_gather(w_out, "section", axis=0, tiled=True),
    )
    projected = jnp.dot(modulated, qkv_full, preferred_element_type=jnp.float32).astype(
        jnp.bfloat16
    )
    grouped = projected.reshape(tok_rows, heads_dev, 3, HEAD_DIM)
    queries = grouped[:, :, 0]
    key_rows = grouped[:, :, 1]
    value_rows = grouped[:, :, 2]
    scale_factor = 1.0 / math.sqrt(HEAD_DIM)
    initial = (
        jnp.full((tok_rows, heads_dev), -1e30, jnp.float32),
        jnp.zeros((tok_rows, heads_dev), jnp.float32),
        jnp.zeros((tok_rows, heads_dev, HEAD_DIM), jnp.float32),
    )
    key_piece = lax.all_gather(key_rows, ("seq", "section"), axis=0, tiled=True)
    value_piece = lax.all_gather(value_rows, ("seq", "section"), axis=0, tiled=True)
    total_rows = key_piece.shape[0]
    block_rows = math.gcd(total_rows, 1024)

    def one_block(block_index, carried_block):
        running, totals, weighted = carried_block
        key_block = lax.dynamic_slice_in_dim(key_piece, block_index * block_rows, block_rows, 0)
        value_block = lax.dynamic_slice_in_dim(value_piece, block_index * block_rows, block_rows, 0)
        scores = (
            jnp.einsum("thd,khd->thk", queries, key_block, preferred_element_type=jnp.float32)
            * scale_factor
        )
        newest = jnp.maximum(running, jnp.max(scores, axis=-1))
        factor = jnp.exp(running - newest)
        weights = jnp.exp(scores - newest[..., None])
        totals = totals * factor + jnp.sum(weights, axis=-1)
        weighted = weighted * factor[..., None] + jnp.einsum(
            "thk,khd->thd",
            weights.astype(jnp.bfloat16),
            value_block,
            preferred_element_type=jnp.float32,
        )
        return (newest, totals, weighted)

    finished = lax.fori_loop(0, total_rows // block_rows, one_block, initial)
    attended = (
        (finished[2] / finished[1][..., None])
        .astype(jnp.bfloat16)
        .reshape(tok_rows, heads_dev * HEAD_DIM)
    )
    mixed_rows = jnp.dot(
        lax.all_gather(attended, "mp", axis=1, tiled=True),
        out_full,
        preferred_element_type=jnp.float32,
    )
    return (latent.astype(jnp.float32) + mod_local[2].astype(jnp.float32) * mixed_rows).astype(
        jnp.bfloat16
    )


def fused_kernel(
    n,
    x_hbm,
    t_ref,
    mod_ref,
    wq_hbm,
    wo_hbm,
    out_ref,
    xs,
    small,
    wq,
    wo,
    acc,
    stat,
    proj,
    pkv,
    att,
    mixed,
    own_sem,
    ssem,
    rsem,
    small_send,
    small_recv,
    wq_sem,
    wq_send,
    wo_sem,
    wo_send,
    kv_send,
    kv_recv,
):
    me = lax.axis_index("mp")
    sec = lax.axis_index("section")
    other = 1 - sec
    deep = n // WIDE
    z, x = me // WIDE, me % WIDE
    rows, feats = x_hbm.shape
    half = rows // 2
    piece_q = wq.shape[1]
    per_sec = n // 2
    piece_o = wo.shape[1]
    heads = att.shape[2] // HEAD_DIM

    own_copy = pltpu.make_async_copy(x_hbm, xs.at[me], own_sem)
    own_copy.start()

    barrier = pltpu.get_barrier_semaphore()
    for step in range(1, n):
        pl.semaphore_signal(
            barrier, inc=1, device_id={"mp": lax.rem(me + step, n)}, device_id_type=MESH
        )
    pl.semaphore_signal(barrier, inc=1, device_id={"section": other}, device_id_type=MESH)

    def wq_local(i):
        p = sec * per_sec + i
        return pltpu.make_async_copy(
            wq_hbm.at[pl.ds(i * piece_q, piece_q)], wq.at[p], wq_sem.at[p]
        )

    def wo_local(i):
        return pltpu.make_async_copy(
            wo_hbm.at[pl.ds(i * piece_o, piece_o)],
            wo.at[sec * per_sec + i],
            wo_sem.at[sec * per_sec + i],
        )

    for i in range(per_sec):
        wq_local(i).start()
    for i in range(per_sec):
        wo_local(i).start()

    own_copy.wait()
    mine = xs[me].astype(jnp.float32)
    mod_f = mod_ref[t_ref[0]].astype(jnp.float32)
    mean_col = jnp.sum(mine, axis=1, keepdims=True) * (1.0 / feats)
    off = mine - mean_col
    m2_col = jnp.sum(off * off, axis=1, keepdims=True)
    mean_row = jnp.broadcast_to(mean_col, (rows, LANES)).T[0:1, :]
    m2_row = jnp.broadcast_to(m2_col, (rows, LANES)).T[0:1, :]
    small[me, 0:1, :] = mod_f[0:1]
    small[me, 1:2, :] = 1.0 + mod_f[1:2]
    small[me, 2:3, 0:rows] = mean_row
    small[me, 3:4, 0:rows] = m2_row

    pl.semaphore_wait(barrier, n)

    def small_copy(step):
        return pltpu.make_async_remote_copy(
            src_ref=small.at[me],
            dst_ref=small.at[me],
            send_sem=small_send.at[step],
            recv_sem=small_recv.at[me],
            device_id={"mp": lax.rem(me + step, n)},
            device_id_type=MESH,
        )

    def chunk(phase, src, h):
        if phase == 0:
            return xs.at[src, pl.ds(h * half, half), :]
        return att.at[src, :, pl.ds(h * HEAD_DIM, HEAD_DIM)]

    def route(src, h):
        sz, sx = src // WIDE, src % WIDE
        same = sx == x
        if h == 0:
            first = jnp.bool_(False)
        else:
            first = jnp.logical_or(sz == 0, sz == deep - 1)
        flow = jnp.logical_or(same, first)
        up = jnp.logical_and(flow, jnp.logical_and(sz <= z, z + 1 < deep))
        down = jnp.logical_and(flow, jnp.logical_and(sz >= z, z > 0))
        across = jnp.logical_and(
            same, jnp.logical_or(jnp.logical_not(first), sz == z)
        )
        return (
            (0, up, me + WIDE),
            (1, down, me - WIDE),
            (2, across, z * WIDE + (1 - x)),
        )

    def hop(phase, src, h, direction, target):
        return pltpu.make_async_remote_copy(
            src_ref=chunk(phase, src, h),
            dst_ref=chunk(phase, src, h),
            send_sem=ssem.at[phase, direction, src, h],
            recv_sem=rsem.at[phase, src, h],
            device_id={"mp": target},
            device_id_type=MESH,
        )

    def relay(phase, src, h):
        for direction, wanted, target in route(src, h):

            @pl.when(wanted)
            def _():
                hop(phase, src, h, direction, target).start()

    def arrive(phase, src, h):
        hop(phase, src, h, 0, me).wait_recv()
        relay(phase, src, h)

    for h in range(2):
        relay(0, me, h)
        if h == 0:
            for step in range(1, n):
                small_copy(step).start()

    def wq_remote(i):
        p = sec * per_sec + i
        return pltpu.make_async_remote_copy(
            src_ref=wq_hbm.at[pl.ds(i * piece_q, piece_q)],
            dst_ref=wq.at[p],
            send_sem=wq_send.at[i],
            recv_sem=wq_sem.at[p],
            device_id={"section": other},
            device_id_type=MESH,
        )

    def wo_remote(i):
        p = sec * per_sec + i
        return pltpu.make_async_remote_copy(
            src_ref=wo_hbm.at[pl.ds(i * piece_o, piece_o)],
            dst_ref=wo.at[p],
            send_sem=wo_send.at[i],
            recv_sem=wo_sem.at[p],
            device_id={"section": other},
            device_id_type=MESH,
        )

    for i in range(per_sec):
        wq_remote(i).start()
    for i in range(per_sec):
        wo_remote(i).start()

    for step in range(1, n):
        p = lax.rem(me + step, n)
        pltpu.make_async_copy(small.at[p], small.at[p], small_recv.at[p]).wait()
    total = jnp.zeros((1, rows), jnp.float32)
    for p in range(n):
        total = total + small[p, 2:3, 0:rows]
    grand = total * (1.0 / n)
    m2 = jnp.zeros((1, rows), jnp.float32)
    for p in range(n):
        gap = small[p, 2:3, 0:rows] - grand
        m2 = m2 + small[p, 3:4, 0:rows] + feats * (gap * gap)
    inv = lax.rsqrt(m2 * (1.0 / (n * feats)) + 1e-06)
    stat[0] = jnp.broadcast_to(grand, (LANES, rows)).T
    stat[1] = jnp.broadcast_to(inv, (LANES, rows)).T

    def project(src):
        pltpu.make_async_copy(wq.at[src], wq.at[src], wq_sem.at[src]).wait()
        mean, rstd = stat[0], stat[1]
        shift_scale = small[src, 0:2, :]
        parts = []
        for c in range(feats // LANES):
            cols = slice(c * LANES, (c + 1) * LANES)
            values = xs[src, :, cols].astype(jnp.float32)
            parts.append(
                ((values - mean) * rstd * shift_scale[1:2, cols] + shift_scale[0:1, cols]).astype(
                    jnp.bfloat16
                )
            )
        return jnp.dot(
            jnp.concatenate(parts, axis=1), wq[src], preferred_element_type=jnp.float32
        )

    acc[...] = project(me)

    def sweep(phase, use):
        def body(d, carry):
            where = []
            for col in (True, False):
                for sign in (1, -1):
                    sz = z + sign * (d if col else d - 1)
                    there = jnp.logical_and(sz >= 0, sz < deep)
                    if not col and sign < 0:
                        there = jnp.logical_and(there, d > 1)
                    where.append((sz * WIDE + (x if col else 1 - x), there))
            for h in range(2):
                for src, there in where:

                    @pl.when(there)
                    def _():
                        arrive(phase, src, h)

            def one(i, carry_in):
                col = i < 2
                sign = 1 - 2 * lax.rem(i, 2)
                sz = z + sign * jnp.where(col, d, d - 1)
                there = jnp.logical_and(sz >= 0, sz < deep)
                there = jnp.logical_and(there, jnp.logical_or(i < 3, d > 1))
                src = sz * WIDE + jnp.where(col, x, 1 - x)

                @pl.when(there)
                def _():
                    use(src)

                return carry_in

            return lax.fori_loop(0, 4, one, carry)

        lax.fori_loop(1, deep + 1, body, 0)

    def use_projection(src):
        acc[...] += project(src)

    sweep(0, use_projection)

    def kv_copy(h):
        return pltpu.make_async_remote_copy(
            src_ref=proj.at[:, pl.ds((3 * h + 1) * HEAD_DIM, 2 * HEAD_DIM)],
            dst_ref=pkv.at[h],
            send_sem=kv_send.at[h],
            recv_sem=kv_recv.at[h],
            device_id={"section": other},
            device_id_type=MESH,
        )

    for h in range(heads):
        cols = slice((3 * h + 1) * HEAD_DIM, (3 * h + 3) * HEAD_DIM)
        proj[:, cols] = acc[:, cols].astype(jnp.bfloat16)
        kv_copy(h).start()

    factor = 1.0 / math.sqrt(HEAD_DIM)
    contract = (((1,), (1,)), ((), ()))
    for h in range(heads):
        base = 3 * h * HEAD_DIM
        queries = acc[:, base : base + HEAD_DIM].astype(jnp.bfloat16)
        own_k = proj[:, base + HEAD_DIM : base + 2 * HEAD_DIM]
        own_v = proj[:, base + 2 * HEAD_DIM : base + 3 * HEAD_DIM]
        s_own = lax.dot_general(queries, own_k, contract, preferred_element_type=jnp.float32) * factor
        kv_copy(h).wait_recv()
        far_k = pkv[h, :, 0:HEAD_DIM]
        far_v = pkv[h, :, HEAD_DIM : 2 * HEAD_DIM]
        s_far = lax.dot_general(queries, far_k, contract, preferred_element_type=jnp.float32) * factor
        top = jnp.maximum(
            jnp.max(s_own, axis=1, keepdims=True), jnp.max(s_far, axis=1, keepdims=True)
        )
        e_own = jnp.exp(s_own - top)
        e_far = jnp.exp(s_far - top)
        norm = jnp.sum(e_own, axis=1, keepdims=True) + jnp.sum(e_far, axis=1, keepdims=True)
        weighted = jnp.dot(
            e_own.astype(jnp.bfloat16), own_v, preferred_element_type=jnp.float32
        ) + jnp.dot(e_far.astype(jnp.bfloat16), far_v, preferred_element_type=jnp.float32)
        att[me, :, h * HEAD_DIM : (h + 1) * HEAD_DIM] = (weighted / norm).astype(jnp.bfloat16)
        relay(1, me, h)

    def mix(src):
        pltpu.make_async_copy(wo.at[src], wo.at[src], wo_sem.at[src]).wait()
        return jnp.dot(att[src], wo[src], preferred_element_type=jnp.float32)

    mixed[...] = mix(me)

    def use_mix(src):
        mixed[...] += mix(src)

    sweep(1, use_mix)

    gate = mod_ref[t_ref[0]].astype(jnp.float32)[2:3]
    out_ref[...] = (xs[me].astype(jnp.float32) + gate * mixed[...]).astype(jnp.bfloat16)

    for step in range(1, n):
        small_copy(step).wait_send()
    for i in range(per_sec):
        wq_remote(i).wait_send()
        wo_remote(i).wait_send()
    for h in range(heads):
        kv_copy(h).wait_send()

    def drain(src, carry):
        for phase in range(2):
            for h in range(2):
                for direction, wanted, target in route(src, h):

                    @pl.when(wanted)
                    def _():
                        hop(phase, src, h, direction, target).wait_send()

        return carry

    lax.fori_loop(0, n, drain, 0)


def fused(n, latent, t_index, mod_table, w_qkv, w_out):
    rows, feats = latent.shape
    depth, cols = w_qkv.shape
    depth_o, cols_o = w_out.shape
    heads = cols // (3 * HEAD_DIM)
    bf, f32 = jnp.bfloat16, jnp.float32
    dma = pltpu.SemaphoreType.DMA
    return pl.pallas_call(
        functools.partial(fused_kernel, n),
        out_shape=jax.ShapeDtypeStruct((rows, feats), bf),
        in_specs=[
            pl.BlockSpec(memory_space=pl.ANY),
            pl.BlockSpec(memory_space=pltpu.SMEM),
            pl.BlockSpec(memory_space=pltpu.VMEM),
            pl.BlockSpec(memory_space=pl.ANY),
            pl.BlockSpec(memory_space=pl.ANY),
        ],
        out_specs=pl.BlockSpec(memory_space=pltpu.VMEM),
        scratch_shapes=[
            pltpu.VMEM((n, rows, feats), bf),
            pltpu.VMEM((n, 8, feats), f32),
            pltpu.VMEM((n, 2 * depth // n, cols), bf),
            pltpu.VMEM((n, 2 * depth_o // n, cols_o), bf),
            pltpu.VMEM((rows, cols), f32),
            pltpu.VMEM((2, rows, LANES), f32),
            pltpu.VMEM((rows, cols), bf),
            pltpu.VMEM((heads, rows, 2 * HEAD_DIM), bf),
            pltpu.VMEM((n, rows, heads * HEAD_DIM), bf),
            pltpu.VMEM((rows, cols_o), f32),
            dma,
            dma((2, 3, n, 2)),
            dma((2, n, 2)),
            dma((n,)),
            dma((n,)),
            dma((n,)),
            dma((n // 2,)),
            dma((n,)),
            dma((n // 2,)),
            dma((heads,)),
            dma((heads,)),
        ],
        compiler_params=pltpu.CompilerParams(
            collective_id=0, has_side_effects=True, vmem_limit_bytes=48 * 1024 * 1024
        ),
    )(latent, t_index, mod_table, w_qkv, w_out)


def solution(mesh):
    in_specs = (
        P(("groups", "seq", "section"), "mp"),
        P("groups"),
        P(None, None, "mp"),
        P("section", "mp"),
        P("section", "mp"),
    )
    out_specs = P(("groups", "seq", "section"), "mp")
    n = mesh.shape["mp"]

    def body(latent, t_index, mod_table, w_qkv, w_out):
        heads = w_qkv.shape[1] // (3 * HEAD_DIM)
        fits = (
            mesh.shape["seq"] == 1
            and mesh.shape["section"] == 2
            and n % WIDE == 0
            and n > WIDE
            and heads == 2
            and latent.shape[0] <= latent.shape[1]
            and latent.shape[0] % 256 == 0
        )
        if not fits:
            return local(latent, t_index, mod_table, w_qkv, w_out)
        return fused(n, latent, t_index, mod_table, w_qkv, w_out)

    return jax.shard_map(body, mesh=mesh, in_specs=in_specs, out_specs=out_specs, check_vma=False)
```

```python
import functools
import math

import jax
import jax.numpy as jnp
from jax import lax
from jax.experimental import pallas as pl
from jax.experimental.pallas import tpu as pltpu
from jax.sharding import PartitionSpec as P

HEAD_DIM = 128
LANES = 128
WIDE = 2
MESH = pl.DeviceIdType.MESH


def layer_normed(values):
    mean_row = jnp.mean(values, axis=-1, keepdims=True)
    centred = values - mean_row
    variance = jnp.mean(centred * centred, axis=-1, keepdims=True)
    return centred * lax.rsqrt(variance + 1e-06)


def local(latent, t_index, mod_table, w_qkv, w_out):
    mod_local = lax.dynamic_index_in_dim(mod_table, t_index[0], 0, keepdims=False)
    features, mod_whole = (
        lax.all_gather(latent, "mp", axis=1, tiled=True),
        lax.all_gather(mod_local, "mp", axis=1, tiled=True),
    )
    mod_float = mod_whole.astype(jnp.float32)
    modulated = (
        layer_normed(features.astype(jnp.float32)) * (1.0 + mod_float[1]) + mod_float[0]
    ).astype(jnp.bfloat16)
    tok_rows = latent.shape[0]
    heads_dev = w_qkv.shape[1] // (3 * HEAD_DIM)
    qkv_full, out_full = (
        lax.all_gather(w_qkv, "section", axis=0, tiled=True),
        lax.all_gather(w_out, "section", axis=0, tiled=True),
    )
    projected = jnp.dot(modulated, qkv_full, preferred_element_type=jnp.float32).astype(
        jnp.bfloat16
    )
    grouped = projected.reshape(tok_rows, heads_dev, 3, HEAD_DIM)
    queries = grouped[:, :, 0]
    key_rows = grouped[:, :, 1]
    value_rows = grouped[:, :, 2]
    scale_factor = 1.0 / math.sqrt(HEAD_DIM)
    initial = (
        jnp.full((tok_rows, heads_dev), -1e30, jnp.float32),
        jnp.zeros((tok_rows, heads_dev), jnp.float32),
        jnp.zeros((tok_rows, heads_dev, HEAD_DIM), jnp.float32),
    )
    key_piece = lax.all_gather(key_rows, ("seq", "section"), axis=0, tiled=True)
    value_piece = lax.all_gather(value_rows, ("seq", "section"), axis=0, tiled=True)
    total_rows = key_piece.shape[0]
    block_rows = math.gcd(total_rows, 1024)

    def one_block(block_index, carried_block):
        running, totals, weighted = carried_block
        key_block = lax.dynamic_slice_in_dim(key_piece, block_index * block_rows, block_rows, 0)
        value_block = lax.dynamic_slice_in_dim(value_piece, block_index * block_rows, block_rows, 0)
        scores = (
            jnp.einsum("thd,khd->thk", queries, key_block, preferred_element_type=jnp.float32)
            * scale_factor
        )
        newest = jnp.maximum(running, jnp.max(scores, axis=-1))
        factor = jnp.exp(running - newest)
        weights = jnp.exp(scores - newest[..., None])
        totals = totals * factor + jnp.sum(weights, axis=-1)
        weighted = weighted * factor[..., None] + jnp.einsum(
            "thk,khd->thd",
            weights.astype(jnp.bfloat16),
            value_block,
            preferred_element_type=jnp.float32,
        )
        return (newest, totals, weighted)

    finished = lax.fori_loop(0, total_rows // block_rows, one_block, initial)
    attended = (
        (finished[2] / finished[1][..., None])
        .astype(jnp.bfloat16)
        .reshape(tok_rows, heads_dev * HEAD_DIM)
    )
    mixed_rows = jnp.dot(
        lax.all_gather(attended, "mp", axis=1, tiled=True),
        out_full,
        preferred_element_type=jnp.float32,
    )
    return (latent.astype(jnp.float32) + mod_local[2].astype(jnp.float32) * mixed_rows).astype(
        jnp.bfloat16
    )


def fused_kernel(
    n,
    x_hbm,
    t_ref,
    mod_hbm,
    wq_hbm,
    wo_hbm,
    out_ref,
    xs,
    table,
    small,
    wq,
    wo,
    acc,
    stat,
    proj,
    pkv,
    att,
    mixed,
    own_sem,
    table_sem,
    ssem,
    rsem,
    small_send,
    small_recv,
    wq_sem,
    wq_send,
    wo_sem,
    wo_send,
    kv_send,
    kv_recv,
):
    me = lax.axis_index("mp")
    sec = lax.axis_index("section")
    other = 1 - sec
    deep = n // WIDE
    z, x = me // WIDE, me % WIDE
    rows, feats = x_hbm.shape
    half = rows // 2
    piece_q = wq.shape[1]
    per_sec = n // 2
    piece_o = wo.shape[1]
    heads = att.shape[2] // HEAD_DIM

    own_copy = pltpu.make_async_copy(x_hbm, xs.at[me], own_sem)
    own_copy.start()
    table_copy = pltpu.make_async_copy(mod_hbm, table, table_sem)
    table_copy.start()

    barrier = pltpu.get_barrier_semaphore()
    for step in range(1, n):
        pl.semaphore_signal(
            barrier, inc=1, device_id={"mp": lax.rem(me + step, n)}, device_id_type=MESH
        )
    pl.semaphore_signal(barrier, inc=1, device_id={"section": other}, device_id_type=MESH)

    def wq_local(i):
        p = sec * per_sec + i
        return pltpu.make_async_copy(
            wq_hbm.at[pl.ds(i * piece_q, piece_q)], wq.at[p], wq_sem.at[p]
        )

    def wo_local(i):
        return pltpu.make_async_copy(
            wo_hbm.at[pl.ds(i * piece_o, piece_o)],
            wo.at[sec * per_sec + i],
            wo_sem.at[sec * per_sec + i],
        )

    for i in range(per_sec):
        wq_local(i).start()
    for i in range(per_sec):
        wo_local(i).start()

    own_copy.wait()
    mine = xs[me].astype(jnp.float32)
    table_copy.wait()

    def mod_row(j):
        entries = table[j].astype(jnp.float32)
        steps = lax.broadcasted_iota(jnp.int32, entries.shape, 0)
        chosen = jnp.where(steps == t_ref[0], entries, 0.0)
        return jnp.sum(chosen, axis=0, keepdims=True)

    mean_col = jnp.sum(mine, axis=1, keepdims=True) * (1.0 / feats)
    off = mine - mean_col
    m2_col = jnp.sum(off * off, axis=1, keepdims=True)
    mean_row = jnp.broadcast_to(mean_col, (rows, LANES)).T[0:1, :]
    m2_row = jnp.broadcast_to(m2_col, (rows, LANES)).T[0:1, :]
    small[me, 0:1, :] = mod_row(0)
    small[me, 1:2, :] = 1.0 + mod_row(1)
    small[me, 2:3, 0:rows] = mean_row
    small[me, 3:4, 0:rows] = m2_row

    pl.semaphore_wait(barrier, n)

    def small_copy(step):
        return pltpu.make_async_remote_copy(
            src_ref=small.at[me],
            dst_ref=small.at[me],
            send_sem=small_send.at[step],
            recv_sem=small_recv.at[me],
            device_id={"mp": lax.rem(me + step, n)},
            device_id_type=MESH,
        )

    def chunk(phase, src, h):
        if phase == 0:
            return xs.at[src, pl.ds(h * half, half), :]
        return att.at[src, :, pl.ds(h * HEAD_DIM, HEAD_DIM)]

    def route(src, h):
        sz, sx = src // WIDE, src % WIDE
        same = sx == x
        if h == 0:
            first = jnp.bool_(False)
        else:
            first = jnp.logical_or(sz == 0, sz == deep - 1)
        flow = jnp.logical_or(same, first)
        up = jnp.logical_and(flow, jnp.logical_and(sz <= z, z + 1 < deep))
        down = jnp.logical_and(flow, jnp.logical_and(sz >= z, z > 0))
        across = jnp.logical_and(
            same, jnp.logical_or(jnp.logical_not(first), sz == z)
        )
        return (
            (0, up, me + WIDE),
            (1, down, me - WIDE),
            (2, across, z * WIDE + (1 - x)),
        )

    def hop(phase, src, h, direction, target):
        return pltpu.make_async_remote_copy(
            src_ref=chunk(phase, src, h),
            dst_ref=chunk(phase, src, h),
            send_sem=ssem.at[phase, direction, src, h],
            recv_sem=rsem.at[phase, src, h],
            device_id={"mp": target},
            device_id_type=MESH,
        )

    def relay(phase, src, h):
        for direction, wanted, target in route(src, h):

            @pl.when(wanted)
            def _():
                hop(phase, src, h, direction, target).start()

    def arrive(phase, src, h):
        hop(phase, src, h, 0, me).wait_recv()
        relay(phase, src, h)

    for h in range(2):
        relay(0, me, h)
        if h == 0:
            for step in range(1, n):
                small_copy(step).start()

    def wq_remote(i):
        p = sec * per_sec + i
        return pltpu.make_async_remote_copy(
            src_ref=wq_hbm.at[pl.ds(i * piece_q, piece_q)],
            dst_ref=wq.at[p],
            send_sem=wq_send.at[i],
            recv_sem=wq_sem.at[p],
            device_id={"section": other},
            device_id_type=MESH,
        )

    def wo_remote(i):
        p = sec * per_sec + i
        return pltpu.make_async_remote_copy(
            src_ref=wo_hbm.at[pl.ds(i * piece_o, piece_o)],
            dst_ref=wo.at[p],
            send_sem=wo_send.at[i],
            recv_sem=wo_sem.at[p],
            device_id={"section": other},
            device_id_type=MESH,
        )

    for i in range(per_sec):
        wq_remote(i).start()
    for i in range(per_sec):
        wo_remote(i).start()

    for step in range(1, n):
        p = lax.rem(me + step, n)
        pltpu.make_async_copy(small.at[p], small.at[p], small_recv.at[p]).wait()
    total = jnp.zeros((1, rows), jnp.float32)
    for p in range(n):
        total = total + small[p, 2:3, 0:rows]
    grand = total * (1.0 / n)
    m2 = jnp.zeros((1, rows), jnp.float32)
    for p in range(n):
        gap = small[p, 2:3, 0:rows] - grand
        m2 = m2 + small[p, 3:4, 0:rows] + feats * (gap * gap)
    inv = lax.rsqrt(m2 * (1.0 / (n * feats)) + 1e-06)
    stat[0] = jnp.broadcast_to(grand, (LANES, rows)).T
    stat[1] = jnp.broadcast_to(inv, (LANES, rows)).T

    def project(src):
        pltpu.make_async_copy(wq.at[src], wq.at[src], wq_sem.at[src]).wait()
        mean, rstd = stat[0], stat[1]
        shift_scale = small[src, 0:2, :]
        parts = []
        for c in range(feats // LANES):
            cols = slice(c * LANES, (c + 1) * LANES)
            values = xs[src, :, cols].astype(jnp.float32)
            parts.append(
                ((values - mean) * rstd * shift_scale[1:2, cols] + shift_scale[0:1, cols]).astype(
                    jnp.bfloat16
                )
            )
        return jnp.dot(
            jnp.concatenate(parts, axis=1), wq[src], preferred_element_type=jnp.float32
        )

    acc[...] = project(me)

    def sweep(phase, use):
        def body(d, carry):
            where = []
            for col in (True, False):
                for sign in (1, -1):
                    sz = z + sign * (d if col else d - 1)
                    there = jnp.logical_and(sz >= 0, sz < deep)
                    if not col and sign < 0:
                        there = jnp.logical_and(there, d > 1)
                    where.append((sz * WIDE + (x if col else 1 - x), there))
            for h in range(2):
                for src, there in where:

                    @pl.when(there)
                    def _():
                        arrive(phase, src, h)

            def one(i, carry_in):
                col = i < 2
                sign = 1 - 2 * lax.rem(i, 2)
                sz = z + sign * jnp.where(col, d, d - 1)
                there = jnp.logical_and(sz >= 0, sz < deep)
                there = jnp.logical_and(there, jnp.logical_or(i < 3, d > 1))
                src = sz * WIDE + jnp.where(col, x, 1 - x)

                @pl.when(there)
                def _():
                    use(src)

                return carry_in

            return lax.fori_loop(0, 4, one, carry)

        lax.fori_loop(1, deep + 1, body, 0)

    def use_projection(src):
        acc[...] += project(src)

    sweep(0, use_projection)

    def kv_copy(h):
        return pltpu.make_async_remote_copy(
            src_ref=proj.at[:, pl.ds((3 * h + 1) * HEAD_DIM, 2 * HEAD_DIM)],
            dst_ref=pkv.at[h],
            send_sem=kv_send.at[h],
            recv_sem=kv_recv.at[h],
            device_id={"section": other},
            device_id_type=MESH,
        )

    for h in range(heads):
        cols = slice((3 * h + 1) * HEAD_DIM, (3 * h + 3) * HEAD_DIM)
        proj[:, cols] = acc[:, cols].astype(jnp.bfloat16)
        kv_copy(h).start()

    factor = 1.0 / math.sqrt(HEAD_DIM)
    contract = (((1,), (1,)), ((), ()))
    for h in range(heads):
        base = 3 * h * HEAD_DIM
        queries = acc[:, base : base + HEAD_DIM].astype(jnp.bfloat16)
        own_k = proj[:, base + HEAD_DIM : base + 2 * HEAD_DIM]
        own_v = proj[:, base + 2 * HEAD_DIM : base + 3 * HEAD_DIM]
        s_own = lax.dot_general(queries, own_k, contract, preferred_element_type=jnp.float32) * factor
        kv_copy(h).wait_recv()
        far_k = pkv[h, :, 0:HEAD_DIM]
        far_v = pkv[h, :, HEAD_DIM : 2 * HEAD_DIM]
        s_far = lax.dot_general(queries, far_k, contract, preferred_element_type=jnp.float32) * factor
        top = jnp.maximum(
            jnp.max(s_own, axis=1, keepdims=True), jnp.max(s_far, axis=1, keepdims=True)
        )
        e_own = jnp.exp(s_own - top)
        e_far = jnp.exp(s_far - top)
        norm = jnp.sum(e_own, axis=1, keepdims=True) + jnp.sum(e_far, axis=1, keepdims=True)
        weighted = jnp.dot(
            e_own.astype(jnp.bfloat16), own_v, preferred_element_type=jnp.float32
        ) + jnp.dot(e_far.astype(jnp.bfloat16), far_v, preferred_element_type=jnp.float32)
        att[me, :, h * HEAD_DIM : (h + 1) * HEAD_DIM] = (weighted / norm).astype(jnp.bfloat16)
        relay(1, me, h)

    def mix(src):
        pltpu.make_async_copy(wo.at[src], wo.at[src], wo_sem.at[src]).wait()
        return jnp.dot(att[src], wo[src], preferred_element_type=jnp.float32)

    mixed[...] = mix(me)

    def use_mix(src):
        mixed[...] += mix(src)

    sweep(1, use_mix)

    gate = mod_row(2)
    out_ref[...] = (xs[me].astype(jnp.float32) + gate * mixed[...]).astype(jnp.bfloat16)

    for step in range(1, n):
        small_copy(step).wait_send()
    for i in range(per_sec):
        wq_remote(i).wait_send()
        wo_remote(i).wait_send()
    for h in range(heads):
        kv_copy(h).wait_send()

    def drain(src, carry):
        for phase in range(2):
            for h in range(2):
                for direction, wanted, target in route(src, h):

                    @pl.when(wanted)
                    def _():
                        hop(phase, src, h, direction, target).wait_send()

        return carry

    lax.fori_loop(0, n, drain, 0)


def fused(n, latent, t_index, mod_table, w_qkv, w_out):
    mod_table = jnp.transpose(mod_table, (1, 0, 2))
    rows, feats = latent.shape
    depth, cols = w_qkv.shape
    depth_o, cols_o = w_out.shape
    heads = cols // (3 * HEAD_DIM)
    bf, f32 = jnp.bfloat16, jnp.float32
    dma = pltpu.SemaphoreType.DMA
    return pl.pallas_call(
        functools.partial(fused_kernel, n),
        out_shape=jax.ShapeDtypeStruct((rows, feats), bf),
        in_specs=[
            pl.BlockSpec(memory_space=pltpu.HBM),
            pl.BlockSpec(memory_space=pltpu.SMEM),
            pl.BlockSpec(memory_space=pltpu.HBM),
            pl.BlockSpec(memory_space=pltpu.HBM),
            pl.BlockSpec(memory_space=pltpu.HBM),
        ],
        out_specs=pl.BlockSpec(memory_space=pltpu.VMEM),
        scratch_shapes=[
            pltpu.VMEM((n, rows, feats), bf),
            pltpu.VMEM(mod_table.shape, bf),
            pltpu.VMEM((n, 8, feats), f32),
            pltpu.VMEM((n, 2 * depth // n, cols), bf),
            pltpu.VMEM((n, 2 * depth_o // n, cols_o), bf),
            pltpu.VMEM((rows, cols), f32),
            pltpu.VMEM((2, rows, LANES), f32),
            pltpu.VMEM((rows, cols), bf),
            pltpu.VMEM((heads, rows, 2 * HEAD_DIM), bf),
            pltpu.VMEM((n, rows, heads * HEAD_DIM), bf),
            pltpu.VMEM((rows, cols_o), f32),
            dma,
            dma,
            dma((2, 3, n, 2)),
            dma((2, n, 2)),
            dma((n,)),
            dma((n,)),
            dma((n,)),
            dma((n // 2,)),
            dma((n,)),
            dma((n // 2,)),
            dma((heads,)),
            dma((heads,)),
        ],
        compiler_params=pltpu.CompilerParams(
            collective_id=0, has_side_effects=True, vmem_limit_bytes=60 * 1024 * 1024
        ),
    )(latent, t_index, mod_table, w_qkv, w_out)


def solution(mesh):
    in_specs = (
        P(("groups", "seq", "section"), "mp"),
        P("groups"),
        P(None, None, "mp"),
        P("section", "mp"),
        P("section", "mp"),
    )
    out_specs = P(("groups", "seq", "section"), "mp")
    n = mesh.shape["mp"]

    def body(latent, t_index, mod_table, w_qkv, w_out):
        heads = w_qkv.shape[1] // (3 * HEAD_DIM)
        fits = (
            mesh.shape["seq"] == 1
            and mesh.shape["section"] == 2
            and n % WIDE == 0
            and n > WIDE
            and heads == 2
            and latent.shape[0] <= latent.shape[1]
            and latent.shape[0] % 256 == 0
        )
        if not fits:
            return local(latent, t_index, mod_table, w_qkv, w_out)
        return fused(n, latent, t_index, mod_table, w_qkv, w_out)

    return jax.shard_map(body, mesh=mesh, in_specs=in_specs, out_specs=out_specs, check_vma=False)
```

```python
import functools
import math

import jax
import jax.numpy as jnp
from jax import lax
from jax.experimental import pallas as pl
from jax.experimental.pallas import tpu as pltpu
from jax.sharding import PartitionSpec as P

HEAD_DIM = 128
LANES = 128
WIDE = 2
MESH = pl.DeviceIdType.MESH


def layer_normed(values):
    mean_row = jnp.mean(values, axis=-1, keepdims=True)
    centred = values - mean_row
    variance = jnp.mean(centred * centred, axis=-1, keepdims=True)
    return centred * lax.rsqrt(variance + 1e-06)


def local(latent, t_index, mod_table, w_qkv, w_out):
    mod_local = lax.dynamic_index_in_dim(mod_table, t_index[0], 0, keepdims=False)
    features, mod_whole = (
        lax.all_gather(latent, "mp", axis=1, tiled=True),
        lax.all_gather(mod_local, "mp", axis=1, tiled=True),
    )
    mod_float = mod_whole.astype(jnp.float32)
    modulated = (
        layer_normed(features.astype(jnp.float32)) * (1.0 + mod_float[1]) + mod_float[0]
    ).astype(jnp.bfloat16)
    tok_rows = latent.shape[0]
    heads_dev = w_qkv.shape[1] // (3 * HEAD_DIM)
    qkv_full, out_full = (
        lax.all_gather(w_qkv, "section", axis=0, tiled=True),
        lax.all_gather(w_out, "section", axis=0, tiled=True),
    )
    projected = jnp.dot(modulated, qkv_full, preferred_element_type=jnp.float32).astype(
        jnp.bfloat16
    )
    grouped = projected.reshape(tok_rows, heads_dev, 3, HEAD_DIM)
    queries = grouped[:, :, 0]
    key_rows = grouped[:, :, 1]
    value_rows = grouped[:, :, 2]
    scale_factor = 1.0 / math.sqrt(HEAD_DIM)
    initial = (
        jnp.full((tok_rows, heads_dev), -1e30, jnp.float32),
        jnp.zeros((tok_rows, heads_dev), jnp.float32),
        jnp.zeros((tok_rows, heads_dev, HEAD_DIM), jnp.float32),
    )
    key_piece = lax.all_gather(key_rows, ("seq", "section"), axis=0, tiled=True)
    value_piece = lax.all_gather(value_rows, ("seq", "section"), axis=0, tiled=True)
    total_rows = key_piece.shape[0]
    block_rows = math.gcd(total_rows, 1024)

    def one_block(block_index, carried_block):
        running, totals, weighted = carried_block
        key_block = lax.dynamic_slice_in_dim(key_piece, block_index * block_rows, block_rows, 0)
        value_block = lax.dynamic_slice_in_dim(value_piece, block_index * block_rows, block_rows, 0)
        scores = (
            jnp.einsum("thd,khd->thk", queries, key_block, preferred_element_type=jnp.float32)
            * scale_factor
        )
        newest = jnp.maximum(running, jnp.max(scores, axis=-1))
        factor = jnp.exp(running - newest)
        weights = jnp.exp(scores - newest[..., None])
        totals = totals * factor + jnp.sum(weights, axis=-1)
        weighted = weighted * factor[..., None] + jnp.einsum(
            "thk,khd->thd",
            weights.astype(jnp.bfloat16),
            value_block,
            preferred_element_type=jnp.float32,
        )
        return (newest, totals, weighted)

    finished = lax.fori_loop(0, total_rows // block_rows, one_block, initial)
    attended = (
        (finished[2] / finished[1][..., None])
        .astype(jnp.bfloat16)
        .reshape(tok_rows, heads_dev * HEAD_DIM)
    )
    mixed_rows = jnp.dot(
        lax.all_gather(attended, "mp", axis=1, tiled=True),
        out_full,
        preferred_element_type=jnp.float32,
    )
    return (latent.astype(jnp.float32) + mod_local[2].astype(jnp.float32) * mixed_rows).astype(
        jnp.bfloat16
    )


def fused_kernel(
    n,
    x_hbm,
    t_ref,
    mod_hbm,
    wq_hbm,
    wo_hbm,
    out_ref,
    xs,
    table,
    small,
    wq,
    wo,
    acc,
    stat,
    proj,
    pkv,
    att,
    mixed,
    own_sem,
    table_sem,
    ssem,
    rsem,
    small_send,
    small_recv,
    wq_sem,
    wq_send,
    wo_sem,
    wo_send,
    kv_send,
    kv_recv,
):
    me = lax.axis_index("mp")
    sec = lax.axis_index("section")
    other = 1 - sec
    deep = n // WIDE
    z, x = me // WIDE, me % WIDE
    rows, feats = x_hbm.shape
    half = rows // 2
    piece_q = wq.shape[1]
    per_sec = n // 2
    piece_o = wo.shape[1]
    heads = att.shape[2] // HEAD_DIM

    own_copy = pltpu.make_async_copy(x_hbm, xs.at[me], own_sem)
    own_copy.start()
    table_copy = pltpu.make_async_copy(mod_hbm, table, table_sem)
    table_copy.start()

    barrier = pltpu.get_barrier_semaphore()
    for step in range(1, n):
        pl.semaphore_signal(
            barrier, inc=1, device_id={"mp": lax.rem(me + step, n)}, device_id_type=MESH
        )
    pl.semaphore_signal(barrier, inc=1, device_id={"section": other}, device_id_type=MESH)

    def wq_local(i):
        p = sec * per_sec + i
        return pltpu.make_async_copy(
            wq_hbm.at[pl.ds(i * piece_q, piece_q)], wq.at[p], wq_sem.at[p]
        )

    def wo_local(i):
        return pltpu.make_async_copy(
            wo_hbm.at[pl.ds(i * piece_o, piece_o)],
            wo.at[sec * per_sec + i],
            wo_sem.at[sec * per_sec + i],
        )

    for i in range(per_sec):
        wq_local(i).start()
    for i in range(per_sec):
        wo_local(i).start()

    own_copy.wait()
    mine = xs[me].astype(jnp.float32)
    table_copy.wait()

    def mod_row(j):
        entries = table[j].astype(jnp.float32)
        steps = lax.broadcasted_iota(jnp.int32, entries.shape, 0)
        chosen = jnp.where(steps == t_ref[0], entries, 0.0)
        return jnp.sum(chosen, axis=0, keepdims=True)

    mean_col = jnp.sum(mine, axis=1, keepdims=True) * (1.0 / feats)
    off = mine - mean_col
    m2_col = jnp.sum(off * off, axis=1, keepdims=True)
    mean_row = jnp.broadcast_to(mean_col, (rows, LANES)).T[0:1, :]
    m2_row = jnp.broadcast_to(m2_col, (rows, LANES)).T[0:1, :]
    small[me, 0:1, :] = mod_row(0)
    small[me, 1:2, :] = 1.0 + mod_row(1)
    small[me, 2:3, 0:rows] = mean_row
    small[me, 3:4, 0:rows] = m2_row

    pl.semaphore_wait(barrier, n)

    def small_copy(step):
        return pltpu.make_async_remote_copy(
            src_ref=small.at[me],
            dst_ref=small.at[me],
            send_sem=small_send.at[step],
            recv_sem=small_recv.at[me],
            device_id={"mp": lax.rem(me + step, n)},
            device_id_type=MESH,
        )

    def chunk(phase, src, h):
        if phase == 0:
            return xs.at[src, pl.ds(h * half, half), :]
        return att.at[src, :, pl.ds(h * HEAD_DIM, HEAD_DIM)]

    def route(src, h):
        sz, sx = src // WIDE, src % WIDE
        same = sx == x
        if h == 0:
            first = jnp.bool_(False)
        else:
            first = jnp.logical_or(sz == 0, sz == deep - 1)
        flow = jnp.logical_or(same, first)
        up = jnp.logical_and(flow, jnp.logical_and(sz <= z, z + 1 < deep))
        down = jnp.logical_and(flow, jnp.logical_and(sz >= z, z > 0))
        across = jnp.logical_and(
            same, jnp.logical_or(jnp.logical_not(first), sz == z)
        )
        return (
            (0, up, me + WIDE),
            (1, down, me - WIDE),
            (2, across, z * WIDE + (1 - x)),
        )

    def hop(phase, src, h, direction, target):
        return pltpu.make_async_remote_copy(
            src_ref=chunk(phase, src, h),
            dst_ref=chunk(phase, src, h),
            send_sem=ssem.at[phase, direction, src, h],
            recv_sem=rsem.at[phase, src, h],
            device_id={"mp": target},
            device_id_type=MESH,
        )

    def relay(phase, src, h):
        for direction, wanted, target in route(src, h):

            @pl.when(wanted)
            def _():
                hop(phase, src, h, direction, target).start()

    def arrive(phase, src, h):
        hop(phase, src, h, 0, me).wait_recv()
        relay(phase, src, h)

    for h in range(2):
        relay(0, me, h)
        if h == 0:
            for step in range(1, n):
                small_copy(step).start()

    def wq_remote(i):
        p = sec * per_sec + i
        return pltpu.make_async_remote_copy(
            src_ref=wq_hbm.at[pl.ds(i * piece_q, piece_q)],
            dst_ref=wq.at[p],
            send_sem=wq_send.at[i],
            recv_sem=wq_sem.at[p],
            device_id={"section": other},
            device_id_type=MESH,
        )

    def wo_remote(i):
        p = sec * per_sec + i
        return pltpu.make_async_remote_copy(
            src_ref=wo_hbm.at[pl.ds(i * piece_o, piece_o)],
            dst_ref=wo.at[p],
            send_sem=wo_send.at[i],
            recv_sem=wo_sem.at[p],
            device_id={"section": other},
            device_id_type=MESH,
        )

    for i in range(per_sec):
        wq_remote(i).start()
    for i in range(per_sec):
        wo_remote(i).start()

    def receive(phase, d):
        where = []
        for col in (True, False):
            for sign in (1, -1):
                sz = z + sign * (d if col else d - 1)
                there = jnp.logical_and(sz >= 0, sz < deep)
                if not col and sign < 0:
                    there = jnp.logical_and(there, d > 1)
                where.append((sz * WIDE + (x if col else 1 - x), there))
        for h in range(2):
            for src, there in where:

                @pl.when(there)
                def _():
                    arrive(phase, src, h)

    def consume(d, use):
        def one(i, carry_in):
            col = i < 2
            sign = 1 - 2 * lax.rem(i, 2)
            sz = z + sign * jnp.where(col, d, d - 1)
            there = jnp.logical_and(sz >= 0, sz < deep)
            there = jnp.logical_and(there, jnp.logical_or(i < 3, d > 1))
            src = sz * WIDE + jnp.where(col, x, 1 - x)

            @pl.when(there)
            def _():
                use(src)

            return carry_in

        lax.fori_loop(0, 4, one, 0)

    def sweep(phase, use):
        def early(d, carry):
            receive(phase, d)
            consume(d - 1, use)
            return carry

        lax.fori_loop(2, deep, early, 0)
        consume(deep - 1, use)
        receive(phase, deep)
        consume(deep, use)

    receive(0, 1)

    for step in range(1, n):
        p = lax.rem(me + step, n)
        pltpu.make_async_copy(small.at[p], small.at[p], small_recv.at[p]).wait()
    total = jnp.zeros((1, rows), jnp.float32)
    for p in range(n):
        total = total + small[p, 2:3, 0:rows]
    grand = total * (1.0 / n)
    m2 = jnp.zeros((1, rows), jnp.float32)
    for p in range(n):
        gap = small[p, 2:3, 0:rows] - grand
        m2 = m2 + small[p, 3:4, 0:rows] + feats * (gap * gap)
    inv = lax.rsqrt(m2 * (1.0 / (n * feats)) + 1e-06)
    stat[0] = jnp.broadcast_to(grand, (LANES, rows)).T
    stat[1] = jnp.broadcast_to(inv, (LANES, rows)).T

    def project(src):
        pltpu.make_async_copy(wq.at[src], wq.at[src], wq_sem.at[src]).wait()
        mean, rstd = stat[0], stat[1]
        shift_scale = small[src, 0:2, :]
        parts = []
        for c in range(feats // LANES):
            cols = slice(c * LANES, (c + 1) * LANES)
            values = xs[src, :, cols].astype(jnp.float32)
            parts.append(
                ((values - mean) * rstd * shift_scale[1:2, cols] + shift_scale[0:1, cols]).astype(
                    jnp.bfloat16
                )
            )
        return jnp.dot(
            jnp.concatenate(parts, axis=1), wq[src], preferred_element_type=jnp.float32
        )

    acc[...] = project(me)

    def use_projection(src):
        acc[...] += project(src)

    sweep(0, use_projection)

    def kv_copy(h):
        return pltpu.make_async_remote_copy(
            src_ref=proj.at[:, pl.ds((3 * h + 1) * HEAD_DIM, 2 * HEAD_DIM)],
            dst_ref=pkv.at[h],
            send_sem=kv_send.at[h],
            recv_sem=kv_recv.at[h],
            device_id={"section": other},
            device_id_type=MESH,
        )

    for h in range(heads):
        cols = slice((3 * h + 1) * HEAD_DIM, (3 * h + 3) * HEAD_DIM)
        proj[:, cols] = acc[:, cols].astype(jnp.bfloat16)
        kv_copy(h).start()

    factor = 1.0 / math.sqrt(HEAD_DIM)
    contract = (((1,), (1,)), ((), ()))
    for h in range(heads):
        base = 3 * h * HEAD_DIM
        queries = acc[:, base : base + HEAD_DIM].astype(jnp.bfloat16)
        own_k = proj[:, base + HEAD_DIM : base + 2 * HEAD_DIM]
        own_v = proj[:, base + 2 * HEAD_DIM : base + 3 * HEAD_DIM]
        s_own = lax.dot_general(queries, own_k, contract, preferred_element_type=jnp.float32) * factor
        kv_copy(h).wait_recv()
        far_k = pkv[h, :, 0:HEAD_DIM]
        far_v = pkv[h, :, HEAD_DIM : 2 * HEAD_DIM]
        s_far = lax.dot_general(queries, far_k, contract, preferred_element_type=jnp.float32) * factor
        top = jnp.maximum(
            jnp.max(s_own, axis=1, keepdims=True), jnp.max(s_far, axis=1, keepdims=True)
        )
        e_own = jnp.exp(s_own - top)
        e_far = jnp.exp(s_far - top)
        norm = jnp.sum(e_own, axis=1, keepdims=True) + jnp.sum(e_far, axis=1, keepdims=True)
        weighted = jnp.dot(
            e_own.astype(jnp.bfloat16), own_v, preferred_element_type=jnp.float32
        ) + jnp.dot(e_far.astype(jnp.bfloat16), far_v, preferred_element_type=jnp.float32)
        att[me, :, h * HEAD_DIM : (h + 1) * HEAD_DIM] = (weighted / norm).astype(jnp.bfloat16)
        relay(1, me, h)

    def mix(src):
        pltpu.make_async_copy(wo.at[src], wo.at[src], wo_sem.at[src]).wait()
        return jnp.dot(att[src], wo[src], preferred_element_type=jnp.float32)

    receive(1, 1)
    mixed[...] = mix(me)

    def use_mix(src):
        mixed[...] += mix(src)

    sweep(1, use_mix)

    gate = mod_row(2)
    out_ref[...] = (xs[me].astype(jnp.float32) + gate * mixed[...]).astype(jnp.bfloat16)

    for step in range(1, n):
        small_copy(step).wait_send()
    for i in range(per_sec):
        wq_remote(i).wait_send()
        wo_remote(i).wait_send()
    for h in range(heads):
        kv_copy(h).wait_send()

    def drain(src, carry):
        for phase in range(2):
            for h in range(2):
                for direction, wanted, target in route(src, h):

                    @pl.when(wanted)
                    def _():
                        hop(phase, src, h, direction, target).wait_send()

        return carry

    lax.fori_loop(0, n, drain, 0)


def fused(n, latent, t_index, mod_table, w_qkv, w_out):
    mod_table = jnp.transpose(mod_table, (1, 0, 2))
    rows, feats = latent.shape
    depth, cols = w_qkv.shape
    depth_o, cols_o = w_out.shape
    heads = cols // (3 * HEAD_DIM)
    bf, f32 = jnp.bfloat16, jnp.float32
    dma = pltpu.SemaphoreType.DMA
    return pl.pallas_call(
        functools.partial(fused_kernel, n),
        out_shape=jax.ShapeDtypeStruct((rows, feats), bf),
        in_specs=[
            pl.BlockSpec(memory_space=pltpu.HBM),
            pl.BlockSpec(memory_space=pltpu.SMEM),
            pl.BlockSpec(memory_space=pltpu.HBM),
            pl.BlockSpec(memory_space=pltpu.HBM),
            pl.BlockSpec(memory_space=pltpu.HBM),
        ],
        out_specs=pl.BlockSpec(memory_space=pltpu.VMEM),
        scratch_shapes=[
            pltpu.VMEM((n, rows, feats), bf),
            pltpu.VMEM(mod_table.shape, bf),
            pltpu.VMEM((n, 8, feats), f32),
            pltpu.VMEM((n, 2 * depth // n, cols), bf),
            pltpu.VMEM((n, 2 * depth_o // n, cols_o), bf),
            pltpu.VMEM((rows, cols), f32),
            pltpu.VMEM((2, rows, LANES), f32),
            pltpu.VMEM((rows, cols), bf),
            pltpu.VMEM((heads, rows, 2 * HEAD_DIM), bf),
            pltpu.VMEM((n, rows, heads * HEAD_DIM), bf),
            pltpu.VMEM((rows, cols_o), f32),
            dma,
            dma,
            dma((2, 3, n, 2)),
            dma((2, n, 2)),
            dma((n,)),
            dma((n,)),
            dma((n,)),
            dma((n // 2,)),
            dma((n,)),
            dma((n // 2,)),
            dma((heads,)),
            dma((heads,)),
        ],
        compiler_params=pltpu.CompilerParams(
            collective_id=0, has_side_effects=True, vmem_limit_bytes=60 * 1024 * 1024
        ),
    )(latent, t_index, mod_table, w_qkv, w_out)


def solution(mesh):
    in_specs = (
        P(("groups", "seq", "section"), "mp"),
        P("groups"),
        P(None, None, "mp"),
        P("section", "mp"),
        P("section", "mp"),
    )
    out_specs = P(("groups", "seq", "section"), "mp")
    n = mesh.shape["mp"]

    def body(latent, t_index, mod_table, w_qkv, w_out):
        heads = w_qkv.shape[1] // (3 * HEAD_DIM)
        fits = (
            mesh.shape["seq"] == 1
            and mesh.shape["section"] == 2
            and n % WIDE == 0
            and n > WIDE
            and heads == 2
            and latent.shape[0] <= latent.shape[1]
            and latent.shape[0] % 256 == 0
        )
        if not fits:
            return local(latent, t_index, mod_table, w_qkv, w_out)
        return fused(n, latent, t_index, mod_table, w_qkv, w_out)

    return jax.shard_map(body, mesh=mesh, in_specs=in_specs, out_specs=out_specs, check_vma=False)
```

```python
import functools
import math

import jax
import jax.numpy as jnp
from jax import lax
from jax.experimental import pallas as pl
from jax.experimental.pallas import tpu as pltpu
from jax.sharding import PartitionSpec as P

HEAD_DIM = 128
LANES = 128
WIDE = 2
CHUNKS = (2, 2)
MESH = pl.DeviceIdType.MESH


def layer_normed(values):
    mean_row = jnp.mean(values, axis=-1, keepdims=True)
    centred = values - mean_row
    variance = jnp.mean(centred * centred, axis=-1, keepdims=True)
    return centred * lax.rsqrt(variance + 1e-06)


def local(latent, t_index, mod_table, w_qkv, w_out):
    mod_local = lax.dynamic_index_in_dim(mod_table, t_index[0], 0, keepdims=False)
    features, mod_whole = (
        lax.all_gather(latent, "mp", axis=1, tiled=True),
        lax.all_gather(mod_local, "mp", axis=1, tiled=True),
    )
    mod_float = mod_whole.astype(jnp.float32)
    modulated = (
        layer_normed(features.astype(jnp.float32)) * (1.0 + mod_float[1]) + mod_float[0]
    ).astype(jnp.bfloat16)
    tok_rows = latent.shape[0]
    heads_dev = w_qkv.shape[1] // (3 * HEAD_DIM)
    qkv_full, out_full = (
        lax.all_gather(w_qkv, "section", axis=0, tiled=True),
        lax.all_gather(w_out, "section", axis=0, tiled=True),
    )
    projected = jnp.dot(modulated, qkv_full, preferred_element_type=jnp.float32).astype(
        jnp.bfloat16
    )
    grouped = projected.reshape(tok_rows, heads_dev, 3, HEAD_DIM)
    queries = grouped[:, :, 0]
    key_rows = grouped[:, :, 1]
    value_rows = grouped[:, :, 2]
    scale_factor = 1.0 / math.sqrt(HEAD_DIM)
    initial = (
        jnp.full((tok_rows, heads_dev), -1e30, jnp.float32),
        jnp.zeros((tok_rows, heads_dev), jnp.float32),
        jnp.zeros((tok_rows, heads_dev, HEAD_DIM), jnp.float32),
    )
    key_piece = lax.all_gather(key_rows, ("seq", "section"), axis=0, tiled=True)
    value_piece = lax.all_gather(value_rows, ("seq", "section"), axis=0, tiled=True)
    total_rows = key_piece.shape[0]
    block_rows = math.gcd(total_rows, 1024)

    def one_block(block_index, carried_block):
        running, totals, weighted = carried_block
        key_block = lax.dynamic_slice_in_dim(key_piece, block_index * block_rows, block_rows, 0)
        value_block = lax.dynamic_slice_in_dim(value_piece, block_index * block_rows, block_rows, 0)
        scores = (
            jnp.einsum("thd,khd->thk", queries, key_block, preferred_element_type=jnp.float32)
            * scale_factor
        )
        newest = jnp.maximum(running, jnp.max(scores, axis=-1))
        factor = jnp.exp(running - newest)
        weights = jnp.exp(scores - newest[..., None])
        totals = totals * factor + jnp.sum(weights, axis=-1)
        weighted = weighted * factor[..., None] + jnp.einsum(
            "thk,khd->thd",
            weights.astype(jnp.bfloat16),
            value_block,
            preferred_element_type=jnp.float32,
        )
        return (newest, totals, weighted)

    finished = lax.fori_loop(0, total_rows // block_rows, one_block, initial)
    attended = (
        (finished[2] / finished[1][..., None])
        .astype(jnp.bfloat16)
        .reshape(tok_rows, heads_dev * HEAD_DIM)
    )
    mixed_rows = jnp.dot(
        lax.all_gather(attended, "mp", axis=1, tiled=True),
        out_full,
        preferred_element_type=jnp.float32,
    )
    return (latent.astype(jnp.float32) + mod_local[2].astype(jnp.float32) * mixed_rows).astype(
        jnp.bfloat16
    )


def fused_kernel(
    n,
    x_hbm,
    t_ref,
    mod_hbm,
    wq_hbm,
    wo_hbm,
    out_ref,
    xs,
    table,
    small,
    wq,
    wo,
    acc,
    stat,
    proj,
    pkv,
    att,
    mixed,
    own_sem,
    table_sem,
    ssem,
    rsem,
    small_send,
    small_recv,
    wq_sem,
    wq_send,
    wo_sem,
    wo_send,
    kv_send,
    kv_recv,
):
    me = lax.axis_index("mp")
    sec = lax.axis_index("section")
    other = 1 - sec
    deep = n // WIDE
    z, x = me // WIDE, me % WIDE
    rows, feats = x_hbm.shape
    piece_q = wq.shape[1]
    per_sec = n // 2
    piece_o = wo.shape[1]
    heads = att.shape[2] // HEAD_DIM

    own_copy = pltpu.make_async_copy(x_hbm, xs.at[me], own_sem)
    own_copy.start()
    table_copy = pltpu.make_async_copy(mod_hbm, table, table_sem)
    table_copy.start()

    barrier = pltpu.get_barrier_semaphore()
    for step in range(1, n):
        pl.semaphore_signal(
            barrier, inc=1, device_id={"mp": lax.rem(me + step, n)}, device_id_type=MESH
        )
    pl.semaphore_signal(barrier, inc=1, device_id={"section": other}, device_id_type=MESH)

    def wq_local(i):
        p = sec * per_sec + i
        return pltpu.make_async_copy(
            wq_hbm.at[pl.ds(i * piece_q, piece_q)], wq.at[p], wq_sem.at[p]
        )

    def wo_local(i):
        return pltpu.make_async_copy(
            wo_hbm.at[pl.ds(i * piece_o, piece_o)],
            wo.at[sec * per_sec + i],
            wo_sem.at[sec * per_sec + i],
        )

    for i in range(per_sec):
        wq_local(i).start()
    for i in range(per_sec):
        wo_local(i).start()

    own_copy.wait()
    mine = xs[me].astype(jnp.float32)
    table_copy.wait()

    def mod_row(j):
        entries = table[j].astype(jnp.float32)
        steps = lax.broadcasted_iota(jnp.int32, entries.shape, 0)
        chosen = jnp.where(steps == t_ref[0], entries, 0.0)
        return jnp.sum(chosen, axis=0, keepdims=True)

    mean_col = jnp.sum(mine, axis=1, keepdims=True) * (1.0 / feats)
    off = mine - mean_col
    m2_col = jnp.sum(off * off, axis=1, keepdims=True)
    mean_row = jnp.broadcast_to(mean_col, (rows, LANES)).T[0:1, :]
    m2_row = jnp.broadcast_to(m2_col, (rows, LANES)).T[0:1, :]
    small[me, 0:1, :] = mod_row(0)
    small[me, 1:2, :] = 1.0 + mod_row(1)
    small[me, 2:3, 0:rows] = mean_row
    small[me, 3:4, 0:rows] = m2_row

    pl.semaphore_wait(barrier, n)

    def small_copy(step):
        return pltpu.make_async_remote_copy(
            src_ref=small.at[me],
            dst_ref=small.at[me],
            send_sem=small_send.at[step],
            recv_sem=small_recv.at[me],
            device_id={"mp": lax.rem(me + step, n)},
            device_id_type=MESH,
        )

    def chunk(phase, src, h):
        if phase == 0:
            part = rows // CHUNKS[0]
            return xs.at[src, pl.ds(h * part, part), :]
        split = CHUNKS[1] // heads
        part = rows // split
        return att.at[
            src, pl.ds(h % split * part, part), pl.ds(h // split * HEAD_DIM, HEAD_DIM)
        ]

    def route(src):
        sz, sx = src // WIDE, src % WIDE
        same = sx == x
        up = jnp.logical_and(same, jnp.logical_and(sz <= z, z + 1 < deep))
        down = jnp.logical_and(same, jnp.logical_and(sz >= z, z > 0))
        across = same
        return (
            (0, up, me + WIDE),
            (1, down, me - WIDE),
            (2, across, z * WIDE + (1 - x)),
        )

    def hop(phase, src, h, direction, target):
        return pltpu.make_async_remote_copy(
            src_ref=chunk(phase, src, h),
            dst_ref=chunk(phase, src, h),
            send_sem=ssem.at[phase, direction, src, h],
            recv_sem=rsem.at[phase, src, h],
            device_id={"mp": target},
            device_id_type=MESH,
        )

    def relay(phase, src, h):
        for direction, wanted, target in route(src):

            @pl.when(wanted)
            def _():
                hop(phase, src, h, direction, target).start()

    def arrive(phase, src, h):
        hop(phase, src, h, 0, me).wait_recv()
        relay(phase, src, h)

    for step in range(1, n):
        small_copy(step).start()
    for h in range(CHUNKS[0]):
        relay(0, me, h)

    def wq_remote(i):
        p = sec * per_sec + i
        return pltpu.make_async_remote_copy(
            src_ref=wq_hbm.at[pl.ds(i * piece_q, piece_q)],
            dst_ref=wq.at[p],
            send_sem=wq_send.at[i],
            recv_sem=wq_sem.at[p],
            device_id={"section": other},
            device_id_type=MESH,
        )

    def wo_remote(i):
        p = sec * per_sec + i
        return pltpu.make_async_remote_copy(
            src_ref=wo_hbm.at[pl.ds(i * piece_o, piece_o)],
            dst_ref=wo.at[p],
            send_sem=wo_send.at[i],
            recv_sem=wo_sem.at[p],
            device_id={"section": other},
            device_id_type=MESH,
        )

    for i in range(per_sec):
        wq_remote(i).start()
    for i in range(per_sec):
        wo_remote(i).start()

    def receive(phase, d):
        where = []
        for sign in (1, -1):
            sz = z + sign * d
            where.append((sz * WIDE + x, jnp.logical_and(sz >= 0, sz < deep)))
        for h in range(CHUNKS[phase]):
            for src, there in where:

                @pl.when(there)
                def _():
                    arrive(phase, src, h)

    def consume(phase, d, use):
        def one(i, carry_in):
            col = i < 2
            sign = 1 - 2 * lax.rem(i, 2)
            sz = z + sign * jnp.where(col, d, d - 1)
            there = jnp.logical_and(sz >= 0, sz < deep)
            there = jnp.logical_and(there, jnp.logical_or(i < 3, d > 1))
            src = sz * WIDE + jnp.where(col, x, 1 - x)

            @pl.when(jnp.logical_and(there, i >= 2))
            def _():
                for h in range(CHUNKS[phase]):
                    hop(phase, src, h, 0, me).wait_recv()

            @pl.when(there)
            def _():
                use(src)

            return carry_in

        lax.fori_loop(0, 4, one, 0)

    def sweep(phase, use):
        def early(d, carry):
            receive(phase, d)
            consume(phase, d - 1, use)
            return carry

        lax.fori_loop(2, deep, early, 0)
        consume(phase, deep - 1, use)
        consume(phase, deep, use)

    receive(0, 1)

    for step in range(1, n):
        p = lax.rem(me + step, n)
        pltpu.make_async_copy(small.at[p], small.at[p], small_recv.at[p]).wait()
    total = jnp.zeros((1, rows), jnp.float32)
    for p in range(n):
        total = total + small[p, 2:3, 0:rows]
    grand = total * (1.0 / n)
    m2 = jnp.zeros((1, rows), jnp.float32)
    for p in range(n):
        gap = small[p, 2:3, 0:rows] - grand
        m2 = m2 + small[p, 3:4, 0:rows] + feats * (gap * gap)
    inv = lax.rsqrt(m2 * (1.0 / (n * feats)) + 1e-06)
    stat[0] = jnp.broadcast_to(grand, (LANES, rows)).T
    stat[1] = jnp.broadcast_to(inv, (LANES, rows)).T

    def project(src):
        pltpu.make_async_copy(wq.at[src], wq.at[src], wq_sem.at[src]).wait()
        mean, rstd = stat[0], stat[1]
        shift_scale = small[src, 0:2, :]
        parts = []
        for c in range(feats // LANES):
            cols = slice(c * LANES, (c + 1) * LANES)
            values = xs[src, :, cols].astype(jnp.float32)
            parts.append(
                ((values - mean) * rstd * shift_scale[1:2, cols] + shift_scale[0:1, cols]).astype(
                    jnp.bfloat16
                )
            )
        return jnp.dot(
            jnp.concatenate(parts, axis=1), wq[src], preferred_element_type=jnp.float32
        )

    acc[...] = project(me)

    def use_projection(src):
        acc[...] += project(src)

    sweep(0, use_projection)

    def kv_copy(h):
        return pltpu.make_async_remote_copy(
            src_ref=proj.at[:, pl.ds((3 * h + 1) * HEAD_DIM, 2 * HEAD_DIM)],
            dst_ref=pkv.at[h],
            send_sem=kv_send.at[h],
            recv_sem=kv_recv.at[h],
            device_id={"section": other},
            device_id_type=MESH,
        )

    for h in range(heads):
        cols = slice((3 * h + 1) * HEAD_DIM, (3 * h + 3) * HEAD_DIM)
        proj[:, cols] = acc[:, cols].astype(jnp.bfloat16)
        kv_copy(h).start()

    factor = 1.0 / math.sqrt(HEAD_DIM)
    contract = (((1,), (1,)), ((), ()))
    for h in range(heads):
        base = 3 * h * HEAD_DIM
        queries = acc[:, base : base + HEAD_DIM].astype(jnp.bfloat16)
        own_k = proj[:, base + HEAD_DIM : base + 2 * HEAD_DIM]
        own_v = proj[:, base + 2 * HEAD_DIM : base + 3 * HEAD_DIM]
        s_own = lax.dot_general(queries, own_k, contract, preferred_element_type=jnp.float32) * factor
        kv_copy(h).wait_recv()
        far_k = pkv[h, :, 0:HEAD_DIM]
        far_v = pkv[h, :, HEAD_DIM : 2 * HEAD_DIM]
        s_far = lax.dot_general(queries, far_k, contract, preferred_element_type=jnp.float32) * factor
        top = jnp.maximum(
            jnp.max(s_own, axis=1, keepdims=True), jnp.max(s_far, axis=1, keepdims=True)
        )
        e_own = jnp.exp(s_own - top)
        e_far = jnp.exp(s_far - top)
        norm = jnp.sum(e_own, axis=1, keepdims=True) + jnp.sum(e_far, axis=1, keepdims=True)
        weighted = jnp.dot(
            e_own.astype(jnp.bfloat16), own_v, preferred_element_type=jnp.float32
        ) + jnp.dot(e_far.astype(jnp.bfloat16), far_v, preferred_element_type=jnp.float32)
        att[me, :, h * HEAD_DIM : (h + 1) * HEAD_DIM] = (weighted / norm).astype(jnp.bfloat16)
        for c in range(CHUNKS[1] // heads):
            relay(1, me, h * (CHUNKS[1] // heads) + c)

    def mix(src):
        pltpu.make_async_copy(wo.at[src], wo.at[src], wo_sem.at[src]).wait()
        return jnp.dot(att[src], wo[src], preferred_element_type=jnp.float32)

    receive(1, 1)
    mixed[...] = mix(me)

    def use_mix(src):
        mixed[...] += mix(src)

    sweep(1, use_mix)

    gate = mod_row(2)
    out_ref[...] = (xs[me].astype(jnp.float32) + gate * mixed[...]).astype(jnp.bfloat16)

    for step in range(1, n):
        small_copy(step).wait_send()
    for i in range(per_sec):
        wq_remote(i).wait_send()
        wo_remote(i).wait_send()
    for h in range(heads):
        kv_copy(h).wait_send()

    def drain(src, carry):
        for phase in range(2):
            for h in range(CHUNKS[phase]):
                for direction, wanted, target in route(src):

                    @pl.when(wanted)
                    def _():
                        hop(phase, src, h, direction, target).wait_send()

        return carry

    lax.fori_loop(0, n, drain, 0)


def fused(n, latent, t_index, mod_table, w_qkv, w_out):
    mod_table = jnp.transpose(mod_table, (1, 0, 2))
    rows, feats = latent.shape
    depth, cols = w_qkv.shape
    depth_o, cols_o = w_out.shape
    heads = cols // (3 * HEAD_DIM)
    bf, f32 = jnp.bfloat16, jnp.float32
    dma = pltpu.SemaphoreType.DMA
    return pl.pallas_call(
        functools.partial(fused_kernel, n),
        out_shape=jax.ShapeDtypeStruct((rows, feats), bf),
        in_specs=[
            pl.BlockSpec(memory_space=pltpu.HBM),
            pl.BlockSpec(memory_space=pltpu.SMEM),
            pl.BlockSpec(memory_space=pltpu.HBM),
            pl.BlockSpec(memory_space=pltpu.HBM),
            pl.BlockSpec(memory_space=pltpu.HBM),
        ],
        out_specs=pl.BlockSpec(memory_space=pltpu.VMEM),
        scratch_shapes=[
            pltpu.VMEM((n, rows, feats), bf),
            pltpu.VMEM(mod_table.shape, bf),
            pltpu.VMEM((n, 8, feats), f32),
            pltpu.VMEM((n, 2 * depth // n, cols), bf),
            pltpu.VMEM((n, 2 * depth_o // n, cols_o), bf),
            pltpu.VMEM((rows, cols), f32),
            pltpu.VMEM((2, rows, LANES), f32),
            pltpu.VMEM((rows, cols), bf),
            pltpu.VMEM((heads, rows, 2 * HEAD_DIM), bf),
            pltpu.VMEM((n, rows, heads * HEAD_DIM), bf),
            pltpu.VMEM((rows, cols_o), f32),
            dma,
            dma,
            dma((2, 3, n, max(CHUNKS))),
            dma((2, n, max(CHUNKS))),
            dma((n,)),
            dma((n,)),
            dma((n,)),
            dma((n // 2,)),
            dma((n,)),
            dma((n // 2,)),
            dma((heads,)),
            dma((heads,)),
        ],
        compiler_params=pltpu.CompilerParams(
            collective_id=0, has_side_effects=True, vmem_limit_bytes=60 * 1024 * 1024
        ),
    )(latent, t_index, mod_table, w_qkv, w_out)


def solution(mesh):
    in_specs = (
        P(("groups", "seq", "section"), "mp"),
        P("groups"),
        P(None, None, "mp"),
        P("section", "mp"),
        P("section", "mp"),
    )
    out_specs = P(("groups", "seq", "section"), "mp")
    n = mesh.shape["mp"]

    def body(latent, t_index, mod_table, w_qkv, w_out):
        heads = w_qkv.shape[1] // (3 * HEAD_DIM)
        fits = (
            mesh.shape["seq"] == 1
            and mesh.shape["section"] == 2
            and n % WIDE == 0
            and n > WIDE
            and heads == 2
            and latent.shape[0] <= latent.shape[1]
            and latent.shape[0] % 256 == 0
        )
        if not fits:
            return local(latent, t_index, mod_table, w_qkv, w_out)
        return fused(n, latent, t_index, mod_table, w_qkv, w_out)

    return jax.shard_map(body, mesh=mesh, in_specs=in_specs, out_specs=out_specs, check_vma=False)
```

```python
import functools
import math

import jax
import jax.numpy as jnp
from jax import lax
from jax.experimental import pallas as pl
from jax.experimental.pallas import tpu as pltpu
from jax.sharding import PartitionSpec as P

HEAD_DIM = 128
LANES = 128
WIDE = 2
CHUNKS = (2, 2)
MESH = pl.DeviceIdType.MESH


def layer_normed(values):
    mean_row = jnp.mean(values, axis=-1, keepdims=True)
    centred = values - mean_row
    variance = jnp.mean(centred * centred, axis=-1, keepdims=True)
    return centred * lax.rsqrt(variance + 1e-06)


def local(latent, t_index, mod_table, w_qkv, w_out):
    mod_local = lax.dynamic_index_in_dim(mod_table, t_index[0], 0, keepdims=False)
    features, mod_whole = (
        lax.all_gather(latent, "mp", axis=1, tiled=True),
        lax.all_gather(mod_local, "mp", axis=1, tiled=True),
    )
    mod_float = mod_whole.astype(jnp.float32)
    modulated = (
        layer_normed(features.astype(jnp.float32)) * (1.0 + mod_float[1]) + mod_float[0]
    ).astype(jnp.bfloat16)
    tok_rows = latent.shape[0]
    heads_dev = w_qkv.shape[1] // (3 * HEAD_DIM)
    qkv_full, out_full = (
        lax.all_gather(w_qkv, "section", axis=0, tiled=True),
        lax.all_gather(w_out, "section", axis=0, tiled=True),
    )
    projected = jnp.dot(modulated, qkv_full, preferred_element_type=jnp.float32).astype(
        jnp.bfloat16
    )
    grouped = projected.reshape(tok_rows, heads_dev, 3, HEAD_DIM)
    queries = grouped[:, :, 0]
    key_rows = grouped[:, :, 1]
    value_rows = grouped[:, :, 2]
    scale_factor = 1.0 / math.sqrt(HEAD_DIM)
    initial = (
        jnp.full((tok_rows, heads_dev), -1e30, jnp.float32),
        jnp.zeros((tok_rows, heads_dev), jnp.float32),
        jnp.zeros((tok_rows, heads_dev, HEAD_DIM), jnp.float32),
    )
    key_piece = lax.all_gather(key_rows, ("seq", "section"), axis=0, tiled=True)
    value_piece = lax.all_gather(value_rows, ("seq", "section"), axis=0, tiled=True)
    total_rows = key_piece.shape[0]
    block_rows = math.gcd(total_rows, 1024)

    def one_block(block_index, carried_block):
        running, totals, weighted = carried_block
        key_block = lax.dynamic_slice_in_dim(key_piece, block_index * block_rows, block_rows, 0)
        value_block = lax.dynamic_slice_in_dim(value_piece, block_index * block_rows, block_rows, 0)
        scores = (
            jnp.einsum("thd,khd->thk", queries, key_block, preferred_element_type=jnp.float32)
            * scale_factor
        )
        newest = jnp.maximum(running, jnp.max(scores, axis=-1))
        factor = jnp.exp(running - newest)
        weights = jnp.exp(scores - newest[..., None])
        totals = totals * factor + jnp.sum(weights, axis=-1)
        weighted = weighted * factor[..., None] + jnp.einsum(
            "thk,khd->thd",
            weights.astype(jnp.bfloat16),
            value_block,
            preferred_element_type=jnp.float32,
        )
        return (newest, totals, weighted)

    finished = lax.fori_loop(0, total_rows // block_rows, one_block, initial)
    attended = (
        (finished[2] / finished[1][..., None])
        .astype(jnp.bfloat16)
        .reshape(tok_rows, heads_dev * HEAD_DIM)
    )
    mixed_rows = jnp.dot(
        lax.all_gather(attended, "mp", axis=1, tiled=True),
        out_full,
        preferred_element_type=jnp.float32,
    )
    return (latent.astype(jnp.float32) + mod_local[2].astype(jnp.float32) * mixed_rows).astype(
        jnp.bfloat16
    )


def fused_kernel(
    n,
    x_hbm,
    t_ref,
    mod_hbm,
    wq_hbm,
    wo_hbm,
    out_ref,
    xs,
    table,
    small,
    wq,
    wo,
    acc,
    stat,
    proj,
    pkv,
    att,
    mixed,
    own_sem,
    table_sem,
    ssem,
    rsem,
    small_send,
    small_recv,
    wq_sem,
    wq_send,
    wo_sem,
    wo_send,
    kv_send,
    kv_recv,
):
    me = lax.axis_index("mp")
    sec = lax.axis_index("section")
    other = 1 - sec
    deep = n // WIDE
    z, x = me // WIDE, me % WIDE
    rows, feats = x_hbm.shape
    piece_q = wq.shape[1]
    per_sec = n // 2
    piece_o = wo.shape[1]
    heads = att.shape[2] // HEAD_DIM

    own_copy = pltpu.make_async_copy(x_hbm, xs.at[me], own_sem)
    own_copy.start()
    table_copy = pltpu.make_async_copy(mod_hbm, table, table_sem)
    table_copy.start()

    barrier = pltpu.get_barrier_semaphore()
    for step in range(1, n):
        pl.semaphore_signal(
            barrier, inc=1, device_id={"mp": lax.rem(me + step, n)}, device_id_type=MESH
        )
    pl.semaphore_signal(barrier, inc=1, device_id={"section": other}, device_id_type=MESH)

    def wq_local(i):
        p = sec * per_sec + i
        return pltpu.make_async_copy(
            wq_hbm.at[pl.ds(i * piece_q, piece_q)], wq.at[p], wq_sem.at[p]
        )

    def wo_local(i):
        return pltpu.make_async_copy(
            wo_hbm.at[pl.ds(i * piece_o, piece_o)],
            wo.at[sec * per_sec + i],
            wo_sem.at[sec * per_sec + i],
        )

    for i in range(per_sec):
        wq_local(i).start()
    for i in range(per_sec):
        wo_local(i).start()

    own_copy.wait()
    mine = xs[me].astype(jnp.float32)
    table_copy.wait()

    def mod_row(j):
        entries = table[j].astype(jnp.float32)
        steps = lax.broadcasted_iota(jnp.int32, entries.shape, 0)
        chosen = jnp.where(steps == t_ref[0], entries, 0.0)
        return jnp.sum(chosen, axis=0, keepdims=True)

    mean_col = jnp.sum(mine, axis=1, keepdims=True) * (1.0 / feats)
    off = mine - mean_col
    m2_col = jnp.sum(off * off, axis=1, keepdims=True)
    mean_row = jnp.broadcast_to(mean_col, (rows, LANES)).T[0:1, :]
    m2_row = jnp.broadcast_to(m2_col, (rows, LANES)).T[0:1, :]
    small[me, 0:1, :] = mod_row(0)
    small[me, 1:2, :] = 1.0 + mod_row(1)
    small[me, 2:3, 0:rows] = mean_row
    small[me, 3:4, 0:rows] = m2_row

    pl.semaphore_wait(barrier, n)

    def small_copy(step):
        return pltpu.make_async_remote_copy(
            src_ref=small.at[me],
            dst_ref=small.at[me],
            send_sem=small_send.at[step],
            recv_sem=small_recv.at[me],
            device_id={"mp": lax.rem(me + step, n)},
            device_id_type=MESH,
        )

    def chunk(phase, src, h):
        if phase == 0:
            part = rows // CHUNKS[0]
            return xs.at[src, pl.ds(h * part, part), :]
        split = CHUNKS[1] // heads
        part = rows // split
        return att.at[
            src, pl.ds(h % split * part, part), pl.ds(h // split * HEAD_DIM, HEAD_DIM)
        ]

    def route(src):
        sz, sx = src // WIDE, src % WIDE
        same = sx == x
        up = jnp.logical_and(same, jnp.logical_and(sz <= z, z + 1 < deep))
        down = jnp.logical_and(same, jnp.logical_and(sz >= z, z > 0))
        across = same
        return (
            (2, across, z * WIDE + (1 - x)),
            (0, up, me + WIDE),
            (1, down, me - WIDE),
        )

    def hop(phase, src, h, direction, target):
        return pltpu.make_async_remote_copy(
            src_ref=chunk(phase, src, h),
            dst_ref=chunk(phase, src, h),
            send_sem=ssem.at[phase, direction, src, h],
            recv_sem=rsem.at[phase, src, h],
            device_id={"mp": target},
            device_id_type=MESH,
        )

    def relay(phase, src, h):
        for direction, wanted, target in route(src):

            @pl.when(wanted)
            def _():
                hop(phase, src, h, direction, target).start()

    def arrive(phase, src, h):
        hop(phase, src, h, 0, me).wait_recv()
        relay(phase, src, h)

    relay(0, me, 0)
    for step in range(1, n):
        small_copy(step).start()
    for h in range(1, CHUNKS[0]):
        relay(0, me, h)

    def wq_remote(i):
        p = sec * per_sec + i
        return pltpu.make_async_remote_copy(
            src_ref=wq_hbm.at[pl.ds(i * piece_q, piece_q)],
            dst_ref=wq.at[p],
            send_sem=wq_send.at[i],
            recv_sem=wq_sem.at[p],
            device_id={"section": other},
            device_id_type=MESH,
        )

    def wo_remote(i):
        p = sec * per_sec + i
        return pltpu.make_async_remote_copy(
            src_ref=wo_hbm.at[pl.ds(i * piece_o, piece_o)],
            dst_ref=wo.at[p],
            send_sem=wo_send.at[i],
            recv_sem=wo_sem.at[p],
            device_id={"section": other},
            device_id_type=MESH,
        )

    for i in range(per_sec):
        wq_remote(i).start()
    for i in range(per_sec):
        wo_remote(i).start()

    def receive(phase, d):
        where = []
        for sign in (1, -1):
            sz = z + sign * d
            where.append((sz * WIDE + x, jnp.logical_and(sz >= 0, sz < deep)))
        for h in range(CHUNKS[phase]):
            for src, there in where:

                @pl.when(there)
                def _():
                    arrive(phase, src, h)

    def consume(phase, d, use):
        def one(i, carry_in):
            col = i < 2
            sign = 1 - 2 * lax.rem(i, 2)
            sz = z + sign * jnp.where(col, d, d - 1)
            there = jnp.logical_and(sz >= 0, sz < deep)
            there = jnp.logical_and(there, jnp.logical_or(i < 3, d > 1))
            src = sz * WIDE + jnp.where(col, x, 1 - x)

            @pl.when(jnp.logical_and(there, i >= 2))
            def _():
                for h in range(CHUNKS[phase]):
                    hop(phase, src, h, 0, me).wait_recv()

            @pl.when(there)
            def _():
                use(src)

            return carry_in

        lax.fori_loop(0, 4, one, 0)

    def sweep(phase, use):
        def early(d, carry):
            receive(phase, d)
            consume(phase, d - 1, use)
            return carry

        lax.fori_loop(2, deep, early, 0)
        consume(phase, deep - 1, use)
        consume(phase, deep, use)

    receive(0, 1)

    for step in range(1, n):
        p = lax.rem(me + step, n)
        pltpu.make_async_copy(small.at[p], small.at[p], small_recv.at[p]).wait()
    total = jnp.zeros((1, rows), jnp.float32)
    for p in range(n):
        total = total + small[p, 2:3, 0:rows]
    grand = total * (1.0 / n)
    m2 = jnp.zeros((1, rows), jnp.float32)
    for p in range(n):
        gap = small[p, 2:3, 0:rows] - grand
        m2 = m2 + small[p, 3:4, 0:rows] + feats * (gap * gap)
    inv = lax.rsqrt(m2 * (1.0 / (n * feats)) + 1e-06)
    stat[0] = jnp.broadcast_to(grand, (LANES, rows)).T
    stat[1] = jnp.broadcast_to(inv, (LANES, rows)).T

    def project(src):
        pltpu.make_async_copy(wq.at[src], wq.at[src], wq_sem.at[src]).wait()
        mean, rstd = stat[0], stat[1]
        shift_scale = small[src, 0:2, :]
        parts = []
        for c in range(feats // LANES):
            cols = slice(c * LANES, (c + 1) * LANES)
            values = xs[src, :, cols].astype(jnp.float32)
            parts.append(
                ((values - mean) * rstd * shift_scale[1:2, cols] + shift_scale[0:1, cols]).astype(
                    jnp.bfloat16
                )
            )
        return jnp.dot(
            jnp.concatenate(parts, axis=1), wq[src], preferred_element_type=jnp.float32
        )

    acc[...] = project(me)

    def use_projection(src):
        acc[...] += project(src)

    sweep(0, use_projection)

    def kv_copy(h):
        return pltpu.make_async_remote_copy(
            src_ref=proj.at[:, pl.ds((3 * h + 1) * HEAD_DIM, 2 * HEAD_DIM)],
            dst_ref=pkv.at[h],
            send_sem=kv_send.at[h],
            recv_sem=kv_recv.at[h],
            device_id={"section": other},
            device_id_type=MESH,
        )

    for h in range(heads):
        cols = slice((3 * h + 1) * HEAD_DIM, (3 * h + 3) * HEAD_DIM)
        proj[:, cols] = acc[:, cols].astype(jnp.bfloat16)
        kv_copy(h).start()

    factor = 1.0 / math.sqrt(HEAD_DIM)
    contract = (((1,), (1,)), ((), ()))
    for h in range(heads):
        base = 3 * h * HEAD_DIM
        queries = acc[:, base : base + HEAD_DIM].astype(jnp.bfloat16)
        own_k = proj[:, base + HEAD_DIM : base + 2 * HEAD_DIM]
        own_v = proj[:, base + 2 * HEAD_DIM : base + 3 * HEAD_DIM]
        s_own = lax.dot_general(queries, own_k, contract, preferred_element_type=jnp.float32) * factor
        kv_copy(h).wait_recv()
        far_k = pkv[h, :, 0:HEAD_DIM]
        far_v = pkv[h, :, HEAD_DIM : 2 * HEAD_DIM]
        s_far = lax.dot_general(queries, far_k, contract, preferred_element_type=jnp.float32) * factor
        top = jnp.maximum(
            jnp.max(s_own, axis=1, keepdims=True), jnp.max(s_far, axis=1, keepdims=True)
        )
        e_own = jnp.exp(s_own - top)
        e_far = jnp.exp(s_far - top)
        norm = jnp.sum(e_own, axis=1, keepdims=True) + jnp.sum(e_far, axis=1, keepdims=True)
        weighted = jnp.dot(
            e_own.astype(jnp.bfloat16), own_v, preferred_element_type=jnp.float32
        ) + jnp.dot(e_far.astype(jnp.bfloat16), far_v, preferred_element_type=jnp.float32)
        att[me, :, h * HEAD_DIM : (h + 1) * HEAD_DIM] = (weighted / norm).astype(jnp.bfloat16)
        for c in range(CHUNKS[1] // heads):
            relay(1, me, h * (CHUNKS[1] // heads) + c)

    def mix(src):
        pltpu.make_async_copy(wo.at[src], wo.at[src], wo_sem.at[src]).wait()
        return jnp.dot(att[src], wo[src], preferred_element_type=jnp.float32)

    receive(1, 1)
    mixed[...] = mix(me)

    def use_mix(src):
        mixed[...] += mix(src)

    sweep(1, use_mix)

    gate = mod_row(2)
    out_ref[...] = (xs[me].astype(jnp.float32) + gate * mixed[...]).astype(jnp.bfloat16)

    for step in range(1, n):
        small_copy(step).wait_send()
    for i in range(per_sec):
        wq_remote(i).wait_send()
        wo_remote(i).wait_send()
    for h in range(heads):
        kv_copy(h).wait_send()

    def drain(src, carry):
        for phase in range(2):
            for h in range(CHUNKS[phase]):
                for direction, wanted, target in route(src):

                    @pl.when(wanted)
                    def _():
                        hop(phase, src, h, direction, target).wait_send()

        return carry

    lax.fori_loop(0, n, drain, 0)


def fused(n, latent, t_index, mod_table, w_qkv, w_out):
    mod_table = jnp.transpose(mod_table, (1, 0, 2))
    rows, feats = latent.shape
    depth, cols = w_qkv.shape
    depth_o, cols_o = w_out.shape
    heads = cols // (3 * HEAD_DIM)
    bf, f32 = jnp.bfloat16, jnp.float32
    dma = pltpu.SemaphoreType.DMA
    return pl.pallas_call(
        functools.partial(fused_kernel, n),
        out_shape=jax.ShapeDtypeStruct((rows, feats), bf),
        in_specs=[
            pl.BlockSpec(memory_space=pltpu.HBM),
            pl.BlockSpec(memory_space=pltpu.SMEM),
            pl.BlockSpec(memory_space=pltpu.HBM),
            pl.BlockSpec(memory_space=pltpu.HBM),
            pl.BlockSpec(memory_space=pltpu.HBM),
        ],
        out_specs=pl.BlockSpec(memory_space=pltpu.VMEM),
        scratch_shapes=[
            pltpu.VMEM((n, rows, feats), bf),
            pltpu.VMEM(mod_table.shape, bf),
            pltpu.VMEM((n, 8, feats), f32),
            pltpu.VMEM((n, 2 * depth // n, cols), bf),
            pltpu.VMEM((n, 2 * depth_o // n, cols_o), bf),
            pltpu.VMEM((rows, cols), f32),
            pltpu.VMEM((2, rows, LANES), f32),
            pltpu.VMEM((rows, cols), bf),
            pltpu.VMEM((heads, rows, 2 * HEAD_DIM), bf),
            pltpu.VMEM((n, rows, heads * HEAD_DIM), bf),
            pltpu.VMEM((rows, cols_o), f32),
            dma,
            dma,
            dma((2, 3, n, max(CHUNKS))),
            dma((2, n, max(CHUNKS))),
            dma((n,)),
            dma((n,)),
            dma((n,)),
            dma((n // 2,)),
            dma((n,)),
            dma((n // 2,)),
            dma((heads,)),
            dma((heads,)),
        ],
        compiler_params=pltpu.CompilerParams(
            collective_id=0, has_side_effects=True, vmem_limit_bytes=60 * 1024 * 1024
        ),
    )(latent, t_index, mod_table, w_qkv, w_out)


def solution(mesh):
    in_specs = (
        P(("groups", "seq", "section"), "mp"),
        P("groups"),
        P(None, None, "mp"),
        P("section", "mp"),
        P("section", "mp"),
    )
    out_specs = P(("groups", "seq", "section"), "mp")
    n = mesh.shape["mp"]

    def body(latent, t_index, mod_table, w_qkv, w_out):
        heads = w_qkv.shape[1] // (3 * HEAD_DIM)
        fits = (
            mesh.shape["seq"] == 1
            and mesh.shape["section"] == 2
            and n % WIDE == 0
            and n > WIDE
            and heads == 2
            and latent.shape[0] <= latent.shape[1]
            and latent.shape[0] % 256 == 0
        )
        if not fits:
            return local(latent, t_index, mod_table, w_qkv, w_out)
        return fused(n, latent, t_index, mod_table, w_qkv, w_out)

    return jax.shard_map(body, mesh=mesh, in_specs=in_specs, out_specs=out_specs, check_vma=False)
```

```python
import functools
import math

import jax
import jax.numpy as jnp
from jax import lax
from jax.experimental import pallas as pl
from jax.experimental.pallas import tpu as pltpu
from jax.sharding import PartitionSpec as P

HEAD_DIM = 128
LANES = 128
WIDE = 2
CHUNKS = (2, 2)
MESH = pl.DeviceIdType.MESH


def layer_normed(values):
    mean_row = jnp.mean(values, axis=-1, keepdims=True)
    centred = values - mean_row
    variance = jnp.mean(centred * centred, axis=-1, keepdims=True)
    return centred * lax.rsqrt(variance + 1e-06)


def local(latent, t_index, mod_table, w_qkv, w_out):
    mod_local = lax.dynamic_index_in_dim(mod_table, t_index[0], 0, keepdims=False)
    features, mod_whole = (
        lax.all_gather(latent, "mp", axis=1, tiled=True),
        lax.all_gather(mod_local, "mp", axis=1, tiled=True),
    )
    mod_float = mod_whole.astype(jnp.float32)
    modulated = (
        layer_normed(features.astype(jnp.float32)) * (1.0 + mod_float[1]) + mod_float[0]
    ).astype(jnp.bfloat16)
    tok_rows = latent.shape[0]
    heads_dev = w_qkv.shape[1] // (3 * HEAD_DIM)
    qkv_full, out_full = (
        lax.all_gather(w_qkv, "section", axis=0, tiled=True),
        lax.all_gather(w_out, "section", axis=0, tiled=True),
    )
    projected = jnp.dot(modulated, qkv_full, preferred_element_type=jnp.float32).astype(
        jnp.bfloat16
    )
    grouped = projected.reshape(tok_rows, heads_dev, 3, HEAD_DIM)
    queries = grouped[:, :, 0]
    key_rows = grouped[:, :, 1]
    value_rows = grouped[:, :, 2]
    scale_factor = 1.0 / math.sqrt(HEAD_DIM)
    initial = (
        jnp.full((tok_rows, heads_dev), -1e30, jnp.float32),
        jnp.zeros((tok_rows, heads_dev), jnp.float32),
        jnp.zeros((tok_rows, heads_dev, HEAD_DIM), jnp.float32),
    )
    key_piece = lax.all_gather(key_rows, ("seq", "section"), axis=0, tiled=True)
    value_piece = lax.all_gather(value_rows, ("seq", "section"), axis=0, tiled=True)
    total_rows = key_piece.shape[0]
    block_rows = math.gcd(total_rows, 1024)

    def one_block(block_index, carried_block):
        running, totals, weighted = carried_block
        key_block = lax.dynamic_slice_in_dim(key_piece, block_index * block_rows, block_rows, 0)
        value_block = lax.dynamic_slice_in_dim(value_piece, block_index * block_rows, block_rows, 0)
        scores = (
            jnp.einsum("thd,khd->thk", queries, key_block, preferred_element_type=jnp.float32)
            * scale_factor
        )
        newest = jnp.maximum(running, jnp.max(scores, axis=-1))
        factor = jnp.exp(running - newest)
        weights = jnp.exp(scores - newest[..., None])
        totals = totals * factor + jnp.sum(weights, axis=-1)
        weighted = weighted * factor[..., None] + jnp.einsum(
            "thk,khd->thd",
            weights.astype(jnp.bfloat16),
            value_block,
            preferred_element_type=jnp.float32,
        )
        return (newest, totals, weighted)

    finished = lax.fori_loop(0, total_rows // block_rows, one_block, initial)
    attended = (
        (finished[2] / finished[1][..., None])
        .astype(jnp.bfloat16)
        .reshape(tok_rows, heads_dev * HEAD_DIM)
    )
    mixed_rows = jnp.dot(
        lax.all_gather(attended, "mp", axis=1, tiled=True),
        out_full,
        preferred_element_type=jnp.float32,
    )
    return (latent.astype(jnp.float32) + mod_local[2].astype(jnp.float32) * mixed_rows).astype(
        jnp.bfloat16
    )


def fused_kernel(
    n,
    x_hbm,
    t_ref,
    mod_hbm,
    wq_hbm,
    wo_hbm,
    out_ref,
    xs,
    table,
    small,
    wq,
    wo,
    acc,
    stat,
    proj,
    pkv,
    att,
    mixed,
    own_sem,
    table_sem,
    ssem,
    rsem,
    small_send,
    small_recv,
    wq_sem,
    wq_send,
    wo_sem,
    wo_send,
    kv_send,
    kv_recv,
):
    me = lax.axis_index("mp")
    sec = lax.axis_index("section")
    other = 1 - sec
    deep = n // WIDE
    z, x = me // WIDE, me % WIDE
    rows, feats = x_hbm.shape
    piece_q = wq.shape[1]
    per_sec = n // 2
    piece_o = wo.shape[1]
    heads = att.shape[2] // HEAD_DIM

    own_copy = pltpu.make_async_copy(x_hbm, xs.at[me], own_sem)
    own_copy.start()
    table_copy = pltpu.make_async_copy(mod_hbm, table, table_sem)
    table_copy.start()

    barrier = pltpu.get_barrier_semaphore()
    for step in range(1, n):
        pl.semaphore_signal(
            barrier, inc=1, device_id={"mp": lax.rem(me + step, n)}, device_id_type=MESH
        )
    pl.semaphore_signal(barrier, inc=1, device_id={"section": other}, device_id_type=MESH)

    def wq_local(i):
        p = sec * per_sec + i
        return pltpu.make_async_copy(
            wq_hbm.at[pl.ds(i * piece_q, piece_q)], wq.at[p], wq_sem.at[p]
        )

    def wo_local(i):
        return pltpu.make_async_copy(
            wo_hbm.at[pl.ds(i * piece_o, piece_o)],
            wo.at[sec * per_sec + i],
            wo_sem.at[sec * per_sec + i],
        )

    for i in range(per_sec):
        wq_local(i).start()
    for i in range(per_sec):
        wo_local(i).start()

    own_copy.wait()
    mine = xs[me].astype(jnp.float32)
    table_copy.wait()

    def mod_row(j):
        entries = table[j].astype(jnp.float32)
        steps = lax.broadcasted_iota(jnp.int32, entries.shape, 0)
        chosen = jnp.where(steps == t_ref[0], entries, 0.0)
        return jnp.sum(chosen, axis=0, keepdims=True)

    mean_col = jnp.sum(mine, axis=1, keepdims=True) * (1.0 / feats)
    off = mine - mean_col
    m2_col = jnp.sum(off * off, axis=1, keepdims=True)
    mean_row = jnp.broadcast_to(mean_col, (rows, LANES)).T[0:1, :]
    m2_row = jnp.broadcast_to(m2_col, (rows, LANES)).T[0:1, :]
    small[me, 0:1, :] = mod_row(0)
    small[me, 1:2, :] = 1.0 + mod_row(1)
    small[me, 2:3, 0:rows] = mean_row
    small[me, 3:4, 0:rows] = m2_row

    pl.semaphore_wait(barrier, n)

    def small_copy(step):
        return pltpu.make_async_remote_copy(
            src_ref=small.at[me],
            dst_ref=small.at[me],
            send_sem=small_send.at[step],
            recv_sem=small_recv.at[me],
            device_id={"mp": lax.rem(me + step, n)},
            device_id_type=MESH,
        )

    def chunk(phase, src, h):
        if phase == 0:
            part = rows // CHUNKS[0]
            return xs.at[src, pl.ds(h * part, part), :]
        split = CHUNKS[1] // heads
        part = rows // split
        return att.at[
            src, pl.ds(h % split * part, part), pl.ds(h // split * HEAD_DIM, HEAD_DIM)
        ]

    def route(src):
        sz, sx = src // WIDE, src % WIDE
        same = sx == x
        up = jnp.logical_and(same, jnp.logical_and(sz <= z, z + 1 < deep))
        down = jnp.logical_and(same, jnp.logical_and(sz >= z, z > 0))
        across = same
        return (
            (2, across, z * WIDE + (1 - x)),
            (0, up, me + WIDE),
            (1, down, me - WIDE),
        )

    def hop(phase, src, h, direction, target):
        return pltpu.make_async_remote_copy(
            src_ref=chunk(phase, src, h),
            dst_ref=chunk(phase, src, h),
            send_sem=ssem.at[phase, direction, src, h],
            recv_sem=rsem.at[phase, src, h],
            device_id={"mp": target},
            device_id_type=MESH,
        )

    def relay(phase, src, h):
        for direction, wanted, target in route(src):

            @pl.when(wanted)
            def _():
                hop(phase, src, h, direction, target).start()

    def arrive(phase, src, h):
        hop(phase, src, h, 0, me).wait_recv()
        relay(phase, src, h)

    relay(0, me, 0)
    for step in range(1, n):
        small_copy(step).start()
    for h in range(1, CHUNKS[0]):
        relay(0, me, h)

    def wq_remote(i):
        p = sec * per_sec + i
        return pltpu.make_async_remote_copy(
            src_ref=wq_hbm.at[pl.ds(i * piece_q, piece_q)],
            dst_ref=wq.at[p],
            send_sem=wq_send.at[i],
            recv_sem=wq_sem.at[p],
            device_id={"section": other},
            device_id_type=MESH,
        )

    def wo_remote(i):
        p = sec * per_sec + i
        return pltpu.make_async_remote_copy(
            src_ref=wo_hbm.at[pl.ds(i * piece_o, piece_o)],
            dst_ref=wo.at[p],
            send_sem=wo_send.at[i],
            recv_sem=wo_sem.at[p],
            device_id={"section": other},
            device_id_type=MESH,
        )

    for i in range(per_sec):
        wq_remote(i).start()
    for i in range(per_sec):
        wo_remote(i).start()

    def receive(phase, d):
        where = []
        for sign in (1, -1):
            sz = z + sign * d
            where.append((sz * WIDE + x, jnp.logical_and(sz >= 0, sz < deep)))
        for h in range(CHUNKS[phase]):
            for src, there in where:

                @pl.when(there)
                def _():
                    arrive(phase, src, h)

    def consume(phase, d, use):
        def one(i, carry_in):
            col = i < 2
            sign = 1 - 2 * lax.rem(i, 2)
            sz = z + sign * jnp.where(col, d, d - 1)
            there = jnp.logical_and(sz >= 0, sz < deep)
            there = jnp.logical_and(there, jnp.logical_or(i < 3, d > 1))
            src = sz * WIDE + jnp.where(col, x, 1 - x)

            @pl.when(jnp.logical_and(there, i >= 2))
            def _():
                for h in range(CHUNKS[phase]):
                    hop(phase, src, h, 0, me).wait_recv()

            @pl.when(there)
            def _():
                use(src)

            return carry_in

        lax.fori_loop(0, 4, one, 0)

    def sweep(phase, use):
        def early(d, carry):
            receive(phase, d)
            consume(phase, d - 1, use)
            return carry

        lax.fori_loop(2, deep, early, 0)
        consume(phase, deep - 1, use)
        consume(phase, deep, use)

    receive(0, 1)

    for step in range(1, n):
        p = lax.rem(me + step, n)
        pltpu.make_async_copy(small.at[p], small.at[p], small_recv.at[p]).wait()
    total = jnp.zeros((1, rows), jnp.float32)
    for p in range(n):
        total = total + small[p, 2:3, 0:rows]
    grand = total * (1.0 / n)
    m2 = jnp.zeros((1, rows), jnp.float32)
    for p in range(n):
        gap = small[p, 2:3, 0:rows] - grand
        m2 = m2 + small[p, 3:4, 0:rows] + feats * (gap * gap)
    inv = lax.rsqrt(m2 * (1.0 / (n * feats)) + 1e-06)
    stat[0] = jnp.broadcast_to(grand, (LANES, rows)).T
    stat[1] = jnp.broadcast_to(inv, (LANES, rows)).T

    def project(src):
        pltpu.make_async_copy(wq.at[src], wq.at[src], wq_sem.at[src]).wait()
        mean, rstd = stat[0], stat[1]
        shift_scale = small[src, 0:2, :]
        parts = []
        for c in range(feats // LANES):
            cols = slice(c * LANES, (c + 1) * LANES)
            values = xs[src, :, cols].astype(jnp.float32)
            parts.append(
                ((values - mean) * rstd * shift_scale[1:2, cols] + shift_scale[0:1, cols]).astype(
                    jnp.bfloat16
                )
            )
        return jnp.dot(
            jnp.concatenate(parts, axis=1), wq[src], preferred_element_type=jnp.float32
        )

    acc[...] = project(me)

    def use_projection(src):
        acc[...] += project(src)

    sweep(0, use_projection)

    def kv_copy(h):
        return pltpu.make_async_remote_copy(
            src_ref=proj.at[:, pl.ds((3 * h + 1) * HEAD_DIM, 2 * HEAD_DIM)],
            dst_ref=pkv.at[h],
            send_sem=kv_send.at[h],
            recv_sem=kv_recv.at[h],
            device_id={"section": other},
            device_id_type=MESH,
        )

    for h in range(heads):
        cols = slice((3 * h + 1) * HEAD_DIM, (3 * h + 3) * HEAD_DIM)
        proj[:, cols] = acc[:, cols].astype(jnp.bfloat16)
        kv_copy(h).start()

    factor = 1.0 / math.sqrt(HEAD_DIM)
    contract = (((1,), (1,)), ((), ()))
    near = []
    for h in range(heads):
        base = 3 * h * HEAD_DIM
        queries = acc[:, base : base + HEAD_DIM].astype(jnp.bfloat16)
        own_k = proj[:, base + HEAD_DIM : base + 2 * HEAD_DIM]
        s_own = lax.dot_general(queries, own_k, contract, preferred_element_type=jnp.float32) * factor
        near.append((queries, s_own))
    for h in range(heads):
        base = 3 * h * HEAD_DIM
        queries, s_own = near[h]
        own_v = proj[:, base + 2 * HEAD_DIM : base + 3 * HEAD_DIM]
        kv_copy(h).wait_recv()
        far_k = pkv[h, :, 0:HEAD_DIM]
        far_v = pkv[h, :, HEAD_DIM : 2 * HEAD_DIM]
        s_far = lax.dot_general(queries, far_k, contract, preferred_element_type=jnp.float32) * factor
        top = jnp.maximum(
            jnp.max(s_own, axis=1, keepdims=True), jnp.max(s_far, axis=1, keepdims=True)
        )
        e_own = jnp.exp(s_own - top)
        e_far = jnp.exp(s_far - top)
        norm = jnp.sum(e_own, axis=1, keepdims=True) + jnp.sum(e_far, axis=1, keepdims=True)
        weighted = jnp.dot(
            e_own.astype(jnp.bfloat16), own_v, preferred_element_type=jnp.float32
        ) + jnp.dot(e_far.astype(jnp.bfloat16), far_v, preferred_element_type=jnp.float32)
        att[me, :, h * HEAD_DIM : (h + 1) * HEAD_DIM] = (weighted / norm).astype(jnp.bfloat16)
        for c in range(CHUNKS[1] // heads):
            relay(1, me, h * (CHUNKS[1] // heads) + c)

    def mix(src):
        pltpu.make_async_copy(wo.at[src], wo.at[src], wo_sem.at[src]).wait()
        return jnp.dot(att[src], wo[src], preferred_element_type=jnp.float32)

    receive(1, 1)
    mixed[...] = mix(me)

    def use_mix(src):
        mixed[...] += mix(src)

    sweep(1, use_mix)

    gate = mod_row(2)
    out_ref[...] = (xs[me].astype(jnp.float32) + gate * mixed[...]).astype(jnp.bfloat16)

    for step in range(1, n):
        small_copy(step).wait_send()
    for i in range(per_sec):
        wq_remote(i).wait_send()
        wo_remote(i).wait_send()
    for h in range(heads):
        kv_copy(h).wait_send()

    def drain(src, carry):
        for phase in range(2):
            for h in range(CHUNKS[phase]):
                for direction, wanted, target in route(src):

                    @pl.when(wanted)
                    def _():
                        hop(phase, src, h, direction, target).wait_send()

        return carry

    lax.fori_loop(0, n, drain, 0)


def fused(n, latent, t_index, mod_table, w_qkv, w_out):
    mod_table = jnp.transpose(mod_table, (1, 0, 2))
    rows, feats = latent.shape
    depth, cols = w_qkv.shape
    depth_o, cols_o = w_out.shape
    heads = cols // (3 * HEAD_DIM)
    bf, f32 = jnp.bfloat16, jnp.float32
    dma = pltpu.SemaphoreType.DMA
    return pl.pallas_call(
        functools.partial(fused_kernel, n),
        out_shape=jax.ShapeDtypeStruct((rows, feats), bf),
        in_specs=[
            pl.BlockSpec(memory_space=pltpu.HBM),
            pl.BlockSpec(memory_space=pltpu.SMEM),
            pl.BlockSpec(memory_space=pltpu.HBM),
            pl.BlockSpec(memory_space=pltpu.HBM),
            pl.BlockSpec(memory_space=pltpu.HBM),
        ],
        out_specs=pl.BlockSpec(memory_space=pltpu.VMEM),
        scratch_shapes=[
            pltpu.VMEM((n, rows, feats), bf),
            pltpu.VMEM(mod_table.shape, bf),
            pltpu.VMEM((n, 8, feats), f32),
            pltpu.VMEM((n, 2 * depth // n, cols), bf),
            pltpu.VMEM((n, 2 * depth_o // n, cols_o), bf),
            pltpu.VMEM((rows, cols), f32),
            pltpu.VMEM((2, rows, LANES), f32),
            pltpu.VMEM((rows, cols), bf),
            pltpu.VMEM((heads, rows, 2 * HEAD_DIM), bf),
            pltpu.VMEM((n, rows, heads * HEAD_DIM), bf),
            pltpu.VMEM((rows, cols_o), f32),
            dma,
            dma,
            dma((2, 3, n, max(CHUNKS))),
            dma((2, n, max(CHUNKS))),
            dma((n,)),
            dma((n,)),
            dma((n,)),
            dma((n // 2,)),
            dma((n,)),
            dma((n // 2,)),
            dma((heads,)),
            dma((heads,)),
        ],
        compiler_params=pltpu.CompilerParams(
            collective_id=0, has_side_effects=True, vmem_limit_bytes=60 * 1024 * 1024
        ),
    )(latent, t_index, mod_table, w_qkv, w_out)


def solution(mesh):
    in_specs = (
        P(("groups", "seq", "section"), "mp"),
        P("groups"),
        P(None, None, "mp"),
        P("section", "mp"),
        P("section", "mp"),
    )
    out_specs = P(("groups", "seq", "section"), "mp")
    n = mesh.shape["mp"]

    def body(latent, t_index, mod_table, w_qkv, w_out):
        heads = w_qkv.shape[1] // (3 * HEAD_DIM)
        fits = (
            mesh.shape["seq"] == 1
            and mesh.shape["section"] == 2
            and n % WIDE == 0
            and n > WIDE
            and heads == 2
            and latent.shape[0] <= latent.shape[1]
            and latent.shape[0] % 256 == 0
        )
        if not fits:
            return local(latent, t_index, mod_table, w_qkv, w_out)
        return fused(n, latent, t_index, mod_table, w_qkv, w_out)

    return jax.shard_map(body, mesh=mesh, in_specs=in_specs, out_specs=out_specs, check_vma=False)
```
